256 devices in a mesh: gz: 8 (over z), rows: 32 (over x, y, core).
Axes of the slice: x: 4, y: 4, z: 8, core: 2. Of those that a mesh axis runs over, the one named last changes fastest.
Arguments:
- sections: bfloat16 [1, 8, 4096, 512], P(None, 'gz', 'rows'), may hold values from -6 to 6
- block_offset: int32 [1, 8, 32, 4], P(None, 'gz', 'rows'), may hold values from -3 to 3
- row_base: int32 [1, 8, 32, 4], P(None, 'gz', 'rows'), may hold values from 0 to 127
- col_base: int32 [1, 8, 32, 4], P(None, 'gz', 'rows'), may hold values from -128 to 127
- fractions: int32 [2, 1, 8, 32, 4], P(None, None, 'gz', 'rows'), may hold values from 0 to 255
- blend: float32 [1, 8], P(None, 'gz'), may hold values from 0.72 to 0.95
- conv_first: bfloat16 [9, 32, 2], replicated, may hold values from -1.5 to 1.5
- bias_first: float32 [32], replicated, may hold values from -3 to 3
- conv_down: bfloat16 [9, 32, 32], replicated, may hold values from -0.375 to 0.375
- bias_down: float32 [32], replicated, may hold values from -3 to 3
- conv_deep: bfloat16 [2, 9, 32, 32], replicated, may hold values from -0.375 to 0.375
- bias_deep: float32 [2, 32], replicated, may hold values from -3 to 3
Outputs:
- features: bfloat16 [1, 8, 32, 2048, 256], P(None, 'gz', None, 'rows')
The draws below stay inside these ranges and needn't reach their ends.
All inputs are finite; a program needn't handle non-finite values.
Results may differ from the reference program's by a relative error of at most 0.001.
The reference program's roundings to bfloat16 on the way count: a program that leaves them out, or rounds other values in their place, can miss the bound.
Values may be sent and summed in bfloat16 or wider, within the bound.
No kernel may reach another device: no remote copies, remote signals or barrier semaphores. Data moves between devices by JAX's collectives and lax.ppermute only.
A program may use at most 128 MiB of HBM per device.

```python
import math
import jax
import jax.numpy as jnp
from jax import lax

BLOCK = 128
REACH = 3
CHANNELS = 32
COL_BLOCKS = 4
CHAINS = 1
SECTIONS = 8
ROW_BLOCKS = 32
HEIGHT = 4096
WIDTH = 512


def touch_ends(entries, key, least, top_value):
    shape = entries.shape
    place = [jax.random.randint(jax.random.fold_in(key, axis), (), 0, shape[axis]) for axis in range(len(shape))]
    entries = entries.at[tuple(place)].set(least)
    longest = shape.index(max(shape))
    place[longest] = (place[longest] + 1) % shape[longest]
    return entries.at[tuple(place)].set(top_value)


def steps_of(stream_key, shape, cuts, least, high):
    def one(position, shards_of):
        draws = jax.random.uniform(jax.random.fold_in(jax.random.fold_in(stream_key, 6), position), (shards_of,), jnp.float32, least / len(cuts), high / len(cuts))
        return jnp.repeat(jnp.exp(draws), shape[position] // shards_of).reshape((-1,) + (1,) * (len(shape) - position - 1))

    loudness = one(*cuts[0])
    for cut in cuts[1:]:
        loudness = loudness * one(*cut)
    return loudness


def noise(rng, dims, scale, bound, cuts=(), kind=jnp.bfloat16):
    factor_of = steps_of(rng, dims, cuts, -0.22, 0.18) if cuts else 1.0
    values = jax.random.normal(rng, dims, jnp.float32) * scale * factor_of
    return jnp.minimum(jnp.maximum(values, -bound), bound).astype(kind)


def setup_inputs(seed: int = 0) -> dict:
    streams_of = jax.random.split(jax.random.key(seed), 13)
    return {
        "sections": noise(streams_of[0], (CHAINS, SECTIONS, HEIGHT, WIDTH), 1.0, 6.0, ((1, 8), (2, 32))),
        "block_offset": touch_ends(jax.random.randint(streams_of[1], (CHAINS, SECTIONS, ROW_BLOCKS, COL_BLOCKS), -REACH, REACH + 1), jax.random.fold_in(streams_of[1], 1), -REACH, REACH).astype(jnp.int32),
        "row_base": touch_ends(jax.random.randint(streams_of[2], (CHAINS, SECTIONS, ROW_BLOCKS, COL_BLOCKS), 0, BLOCK), jax.random.fold_in(streams_of[2], 1), 0, BLOCK - 1).astype(jnp.int32),
        "col_base": touch_ends(jax.random.randint(streams_of[3], (CHAINS, SECTIONS, ROW_BLOCKS, COL_BLOCKS), -BLOCK, BLOCK), jax.random.fold_in(streams_of[3], 1), -BLOCK, BLOCK - 1).astype(jnp.int32),
        "fractions": touch_ends(jax.random.randint(streams_of[4], (2, CHAINS, SECTIONS, ROW_BLOCKS, COL_BLOCKS), 0, 256), jax.random.fold_in(streams_of[4], 1), 0, 255).astype(jnp.int32),
        "blend": jnp.clip(jnp.exp(math.log(0.95) - 0.2772107 * jax.random.uniform(streams_of[5], (CHAINS, SECTIONS), jnp.float32) ** steps_of(streams_of[5], (CHAINS, SECTIONS), ((1, 8),), -0.2, 0.2)), 0.72, 0.95),
        "conv_first": noise(streams_of[6], (9, CHANNELS, 2), 18 ** -0.5, 1.5),
        "bias_first": noise(streams_of[7], (CHANNELS,), 0.5, 3.0, (), jnp.float32),
        "conv_down": noise(streams_of[8], (9, CHANNELS, CHANNELS), (9 * CHANNELS) ** -0.5, 0.375),
        "bias_down": noise(streams_of[9], (CHANNELS,), 0.5, 3.0, (), jnp.float32),
        "conv_deep": noise(streams_of[10], (2, 9, CHANNELS, CHANNELS), (9 * CHANNELS) ** -0.5, 0.375),
        "bias_deep": noise(streams_of[11], (2, CHANNELS), 0.5, 3.0, (), jnp.float32),
    }


def interp_rows(row_start, fraction):
    weight_hi = fraction.astype(jnp.float32) / 256.0
    out_idx = jnp.arange(BLOCK, dtype=jnp.int32)[:, None]
    src_idx = jnp.arange(2 * BLOCK, dtype=jnp.int32)[None, :]
    matrix = jnp.where(src_idx == out_idx + row_start, 1.0 - weight_hi, 0.0)
    matrix = matrix + jnp.where(src_idx == out_idx + row_start + 1, weight_hi, 0.0)
    return matrix.astype(jnp.bfloat16)


def interp_cols(fraction):
    weight_hi = fraction.astype(jnp.float32) / 256.0
    src_idx = jnp.arange(2 * BLOCK, dtype=jnp.int32)[:, None]
    out_idx = jnp.arange(BLOCK, dtype=jnp.int32)[None, :]
    matrix = jnp.where(src_idx == out_idx, 1.0 - weight_hi, 0.0)
    matrix = matrix + jnp.where(src_idx == out_idx + 1, weight_hi, 0.0)
    return matrix.astype(jnp.bfloat16)


def warp_one(padded, row_idx, col_idx, offset, row_start, col_start, frac_row, frac_col):
    first_row = ((row_idx + offset + REACH) * BLOCK).astype(jnp.int32)
    first_col = (col_idx * BLOCK + col_start + BLOCK).astype(jnp.int32)
    window = lax.dynamic_slice(padded, (first_row, first_col), (2 * BLOCK, 2 * BLOCK))
    moved_cols = jnp.dot(window, interp_cols(frac_col), preferred_element_type=jnp.float32).astype(jnp.bfloat16)
    return jnp.dot(interp_rows(row_start, frac_row), moved_cols, preferred_element_type=jnp.float32)


def warp_section(section, offset, row_start, col_start, fraction):
    padded = jnp.pad(section, ((REACH * BLOCK, (REACH + 1) * BLOCK), (BLOCK, 2 * BLOCK)))
    row_ids = jnp.broadcast_to(jnp.arange(ROW_BLOCKS, dtype=jnp.int32)[:, None], (ROW_BLOCKS, COL_BLOCKS)).reshape(-1)
    col_ids = jnp.broadcast_to(jnp.arange(COL_BLOCKS, dtype=jnp.int32)[None, :], (ROW_BLOCKS, COL_BLOCKS)).reshape(-1)
    blocks = jax.vmap(warp_one, in_axes=(None, 0, 0, 0, 0, 0, 0, 0))(
        padded, row_ids, col_ids, offset.reshape(-1), row_start.reshape(-1), col_start.reshape(-1),
        fraction[0].reshape(-1), fraction[1].reshape(-1))
    return blocks.reshape(ROW_BLOCKS, COL_BLOCKS, BLOCK, BLOCK).transpose(0, 2, 1, 3).reshape(HEIGHT, WIDTH)


def convolve(operand, kernel, stride, padding):
    weights = kernel.astype(jnp.float32).reshape(3, 3, kernel.shape[1], kernel.shape[2]).transpose(2, 3, 0, 1)
    result = lax.conv_general_dilated(operand.astype(jnp.float32)[None], weights, (stride, stride), padding,
                                      precision=lax.Precision.HIGHEST)
    return result[0]


def encode(warped_one, prior_one, conv_first, bias_first, conv_down, bias_down, conv_deep, bias_deep):
    same_pad = ((1, 1), (1, 1))
    encoder_in = jnp.stack([warped_one, prior_one]).astype(jnp.bfloat16)
    hidden = jax.nn.relu(convolve(encoder_in, conv_first, 1, same_pad) + bias_first[:, None, None]).astype(jnp.bfloat16)
    down = jax.nn.relu(convolve(hidden, conv_down, 2, ((1, 0), (1, 0))) + bias_down[:, None, None]).astype(jnp.bfloat16)
    deep = jax.nn.relu(convolve(down, conv_deep[0], 1, same_pad) + bias_deep[0][:, None, None]).astype(jnp.bfloat16)
    return (convolve(deep, conv_deep[1], 1, same_pad) + bias_deep[1][:, None, None]).astype(jnp.bfloat16)


def reference(sections, block_offset, row_base, col_base, fractions, blend, conv_first, bias_first, conv_down, bias_down, conv_deep, bias_deep):
    def one_chain(inputs):
        section_set, offsets, row_starts, col_starts, frac_set, decay = inputs
        warped = lax.map(lambda element: warp_section(*element), (section_set, offsets, row_starts, col_starts, frac_set))

        def blend_step(prior_ref, element):
            decay_rate, section = element
            return decay_rate * prior_ref + (1.0 - decay_rate) * section, prior_ref

        _, priors = lax.scan(blend_step, jnp.zeros((HEIGHT, WIDTH), jnp.float32), (decay, warped))
        return lax.map(lambda element: encode(element[0], element[1], conv_first, bias_first, conv_down, bias_down, conv_deep, bias_deep), (warped, priors))

    return lax.map(one_chain, (sections, block_offset, row_base, col_base, fractions.transpose(1, 2, 0, 3, 4), blend))
```

```python
import jax
import jax.numpy as jnp
from jax import lax
from jax.experimental import pallas as pl
from jax.experimental.pallas import tpu as pltpu
from jax.sharding import PartitionSpec as P

F32 = jnp.float32
BF16 = jnp.bfloat16
VMEM = pltpu.VMEM


def vspec():
    return pl.BlockSpec(memory_space=pltpu.VMEM)


def sspec():
    return pl.BlockSpec(memory_space=pltpu.SMEM)


def aspec():
    return pl.BlockSpec(memory_space=pl.ANY)


def iota(shape, dim):
    return lax.broadcasted_iota(jnp.int32, shape, dim)


def weights_kernel(kf, kd, kp, bf, bd, bp, w1, wd, wp, bb):
    row = iota((32, 256), 0)
    lane = iota((32, 256), 1)

    def place(dr):
        return jnp.where(lane == row + 32 * dr, 1.0, 0.0).astype(BF16)

    spots = [place(dr) for dr in range(3)]

    def base(taps):
        return sum(jnp.dot(taps[dr], spots[dr], preferred_element_type=F32) for dr in range(3))

    within = lane & 31
    quarter = (lane >> 5) & 3
    for phase in range(2):
        acc = jnp.zeros((32, 256), F32)
        for dr in range(3):
            for dx in range(3):
                tap = kf[3 * dr + dx].astype(F32)
                value = jnp.where(lane < 128, tap[:, 0:1], tap[:, 1:2])
                hit = (quarter == dx + phase) & (within == 10 + dr)
                acc = acc + jnp.where(hit, value, 0.0)
        for r in range(16):
            moved = acc if r == 0 else pltpu.roll(acc, r, 1)
            w1[pl.ds(phase * 512 + r * 32, 32), :] = moved.astype(BF16)
    for place_at, dx in enumerate((1, 0, 2)):
        acc = base([kd[3 * dr + dx] for dr in range(3)])
        for r in range(3):
            moved = acc if r == 0 else pltpu.roll(acc, 64 * r, 1)
            wd[pl.ds(place_at * 96 + r * 32, 32), :] = moved.astype(BF16)
    for layer in range(2):
        for dx in range(3):
            acc = base([kp[layer, 3 * dr + dx] for dr in range(3)])
            for r in range(6):
                moved = acc if r == 0 else pltpu.roll(acc, 32 * r, 1)
                wp[layer, pl.ds(dx * 192 + r * 32, 32), :] = moved.astype(BF16)
    diagonal = iota((32, 32), 0) == iota((32, 32), 1)
    for k, line in enumerate((bf[...], bd[...], bp[0:1, :], bp[1:2, :])):
        column = jnp.sum(jnp.where(diagonal, line, 0.0), axis=1, keepdims=True)
        bb[k] = jnp.broadcast_to(column, (32, 256))


def make_weights(conv_first, conv_down, conv_deep, bias_first, bias_down, bias_deep):
    return pl.pallas_call(
        weights_kernel,
        out_shape=(
            jax.ShapeDtypeStruct((1024, 256), BF16),
            jax.ShapeDtypeStruct((288, 256), BF16),
            jax.ShapeDtypeStruct((2, 576, 256), BF16),
            jax.ShapeDtypeStruct((4, 32, 256), F32),
        ),
        in_specs=[vspec()] * 6,
        out_specs=(vspec(),) * 4,
        cost_estimate=pl.CostEstimate(flops=20_000_000, bytes_accessed=2_000_000, transcendentals=0),
        name="weights",
    )(conv_first, conv_down, conv_deep, bias_first[None], bias_down[None], bias_deep)


OFFSETS = (0, 1, 2, -1, -2, 3, 4, -3, -4)


def warp_kernel(offs, base, cols, frac, blend, *refs):
    blocks, (pay, enc, S, MJ, MV, sems) = refs[:9], refs[9:]
    core = lax.rem(lax.axis_index("rows"), 2)
    sign = 1 - 2 * core
    copies = []
    for k, off in enumerate(OFFSETS):
        copies.append(pltpu.make_async_copy(blocks[k], S.at[4 + sign * off], sems.at[k]))
    for copy in copies:
        copy.start()
    mats = []
    for j in range(4):
        lo, hi = max(j - 1, 0), min(j + 1, 3)
        wide = (hi - lo + 1) * 128
        src = iota((wide, 128), 0) + (lo - j) * 128
        n = iota((wide, 128), 1)
        if j % 2 == 0:
            x = jnp.where(n < 64, 2 * n, 2 * n - 127)
        else:
            x = jnp.where(n < 64, 2 * n + 1, 2 * n - 128)
        q = frac[1, 0, 0, 0, j].astype(F32) * (1.0 / 256.0)
        target = cols[0, 0, 0, j] + x
        mat = jnp.where(src == target, 1.0 - q, 0.0) + jnp.where(src == target + 1, q, 0.0)
        mats.append(mat.astype(BF16))
    for copy in copies:
        copy.wait()
    for j in range(4):
        lo, hi = max(j - 1, 0), min(j + 1, 3)
        o = offs[0, 0, 0, j]
        for half in range(2):
            window = S[o + 4 + half, :, lo * 128 : (hi + 1) * 128]
            out = jnp.dot(window, mats[j], preferred_element_type=F32)
            MJ[j, half * 128 : (half + 1) * 128, :] = out.astype(BF16).astype(F32)
    lane1 = iota((136, 128), 1)
    for pair in range(2):
        a = MJ[2 * pair, pl.ds(base[0, 0, 0, 2 * pair], 136), :]
        b = MJ[2 * pair + 1, pl.ds(base[0, 0, 0, 2 * pair + 1], 136), :]
        MV[:, pair * 128 : (pair + 1) * 128] = jnp.where(lane1 < 64, a, b)
        MV[:, 256 + pair * 128 : 256 + (pair + 1) * 128] = pltpu.roll(
            jnp.where(lane1 < 64, b, a), 64, 1
        )
    lane = iota((8, 512), 1)
    row = iota((8, 512), 0)
    which = (lane >> 6) & 3
    p = jnp.zeros((8, 512), F32)
    for j in range(4):
        p = jnp.where(which == j, frac[0, 0, 0, 0, j].astype(F32) * (1.0 / 256.0), p)
    rate = jnp.full((8, 512), blend[0, 0], F32)
    top = rate.astype(BF16).astype(F32)
    mid = (rate - top).astype(BF16).astype(F32)
    low = rate - top - mid
    extra = jnp.where(row == 1, p, jnp.where(row == 2, top, jnp.where(row == 3, mid, low)))
    extra = jnp.where(row > 4, 0.0, extra)
    p16 = jnp.concatenate([p, p], axis=0)
    for k in range(8):
        here = MV[16 * k : 16 * k + 16, :]
        below = MV[16 * k + 1 : 16 * k + 17, :]
        enc[16 * k : 16 * k + 16, :] = ((1.0 - p16) * here + p16 * below).astype(BF16)
        pay[k, 0:16, :] = here.astype(BF16)
        tail = MV[16 * k + 16 : 16 * k + 24, :]
        pay[k, 16:24, :] = jnp.where(row == 0, tail, extra).astype(BF16)


def make_warp(offs, base, cols, frac, blend, blocks):
    return pl.pallas_call(
        warp_kernel,
        out_shape=(
            jax.ShapeDtypeStruct((8, 24, 512), BF16),
            jax.ShapeDtypeStruct((128, 512), BF16),
        ),
        in_specs=[sspec()] * 5 + [aspec()] * 9,
        out_specs=(vspec(), vspec()),
        scratch_shapes=[
            VMEM((9, 128, 512), BF16),
            VMEM((4, 264, 128), F32),
            VMEM((136, 512), F32),
            pltpu.SemaphoreType.DMA((9,)),
        ],
        name="warp",
    )(offs, base, cols, frac, blend, *blocks)


def prior_kernel(got, out, M):
    state = jnp.zeros((16, 512), F32)
    for s in range(8):
        out[s] = state.astype(BF16)
        if s == 7:
            break
        M[s] = got[s].astype(F32)
        p = M[s, 17:18, :]
        rate = M[s, 18:19, :] + M[s, 19:20, :] + M[s, 20:21, :]
        warped = (1.0 - p) * M[s, 0:16, :] + p * M[s, 1:17, :]
        state = rate * state + (1.0 - rate) * warped


def make_prior(got):
    return pl.pallas_call(
        prior_kernel,
        out_shape=jax.ShapeDtypeStruct((8, 16, 512), BF16),
        in_specs=[vspec()],
        out_specs=vspec(),
        scratch_shapes=[VMEM((7, 24, 512), F32)],
        name="prior",
    )(got)


def encoder_kernel(enc, prior, inner, outer, w1, wd, wp, bb, out, AF, HE, HO, D, T, FS):
    place = lax.axis_index("rows")
    core = lax.rem(place, 2)
    is_top = core == 0
    lane = iota((16, 256), 1)
    zeros8 = jnp.zeros((8, 512), F32)

    def fill(ch, tile, value):
        even, odd = value[:, :256], value[:, 256:]
        rows = pl.ds(16 * tile, 16)
        AF[4 * ch, rows, :] = jnp.where(lane == 0, 0.0, pltpu.roll(odd, 1, 1)).astype(BF16)
        AF[4 * ch + 1, rows, :] = even.astype(BF16)
        AF[4 * ch + 2, rows, :] = odd.astype(BF16)
        AF[4 * ch + 3, rows, :] = jnp.where(lane == 255, 0.0, pltpu.roll(even, 255, 1)).astype(BF16)

    for ch in range(2):
        a = inner[ch].astype(F32)
        b = outer[ch].astype(F32)
        above = jnp.where(is_top, b[8:16], a[8:16])
        below = jnp.where(is_top, a[0:8], b[0:8])
        fill(ch, 0, jnp.concatenate([zeros8, above], axis=0))
        fill(ch, 9, jnp.concatenate([below, zeros8], axis=0))
    for k in range(8):
        fill(0, k + 1, enc[16 * k : 16 * k + 16, :].astype(F32))
        fill(1, k + 1, prior[k].astype(F32))

    def spread(k, n):
        return jnp.concatenate([bb[k]] * n, axis=0)

    bias16 = spread(0, 16)
    for g in range(9):
        data = AF[:, 16 * g : 16 * g + 32, :].reshape(256, 256)
        for phase, H in enumerate((HE, HO)):
            got = jnp.dot(w1[512 * phase : 512 * phase + 512, :], data, preferred_element_type=F32)
            H[512 * g : 512 * g + 512, :] = jnp.maximum(got + bias16, 0.0).astype(BF16)

    @pl.when(place == 0)
    def _():
        HE[0:160, :] = jnp.zeros((160, 256), BF16)
        HO[0:160, :] = jnp.zeros((160, 256), BF16)

    @pl.when(place == 31)
    def _():
        HE[4256:4608, :] = jnp.zeros((352, 256), BF16)
        HO[4256:4608, :] = jnp.zeros((352, 256), BF16)

    def right(v):
        at = iota(v.shape, 1)
        return jnp.where(at == 0, 0.0, pltpu.roll(v, 1, 1))

    def left(v):
        at = iota(v.shape, 1)
        return jnp.where(at == 255, 0.0, pltpu.roll(v, 255, 1))

    bias3 = spread(1, 3)
    for g in range(23):
        even = jnp.dot(wd[0:96, :], HE[192 * g : 192 * g + 256, :], preferred_element_type=F32)
        odd = jnp.dot(wd[96:288, :], HO[192 * g : 192 * g + 256, :], preferred_element_type=F32)
        total = even + right(odd[0:96]) + odd[96:192] + bias3
        D[96 * g : 96 * g + 96, :] = jnp.maximum(total, 0.0).astype(BF16)

    @pl.when(place == 0)
    def _():
        D[0:64, :] = jnp.zeros((64, 256), BF16)

    @pl.when(place == 31)
    def _():
        D[2112:2208, :] = jnp.zeros((96, 256), BF16)

    bias6 = spread(2, 6)
    for g in range(11):
        got = jnp.dot(wp[0], D[192 * g : 192 * g + 256, :], preferred_element_type=F32)
        total = got[192:384] + right(got[0:192]) + left(got[384:576]) + bias6
        T[192 * g : 192 * g + 192, :] = jnp.maximum(total, 0.0).astype(BF16)
    T[2112:2176, :] = jnp.zeros((64, 256), BF16)

    @pl.when(place == 0)
    def _():
        T[0:32, :] = jnp.zeros((32, 256), BF16)

    @pl.when(place == 31)
    def _():
        T[2080:2112, :] = jnp.zeros((32, 256), BF16)

    bias7 = spread(3, 6)
    for g in range(11):
        got = jnp.dot(wp[1], T[192 * g : 192 * g + 256, :], preferred_element_type=F32)
        total = got[192:384] + right(got[0:192]) + left(got[384:576]) + bias7
        for half in range(2):
            FS[half, 192 * g : 192 * g + 192, :] = total[:, 128 * half : 128 * half + 128]
    for ch in range(32):
        for half in range(2):
            out[0, 0, ch, :, 128 * half : 128 * half + 128] = FS[
                half, pl.ds(ch, 64, stride=32), :
            ].astype(BF16)


def make_encoder(enc, prior, inner, outer, w1, wd, wp, bb):
    return pl.pallas_call(
        encoder_kernel,
        out_shape=jax.ShapeDtypeStruct((1, 1, 32, 64, 256), BF16),
        in_specs=[vspec()] * 8,
        out_specs=vspec(),
        scratch_shapes=[
            VMEM((8, 160, 256), BF16),
            VMEM((4608, 256), BF16),
            VMEM((4608, 256), BF16),
            VMEM((2208, 256), BF16),
            VMEM((2176, 256), BF16),
            VMEM((2, 2112, 128), F32),
        ],
        name="encoder",
    )(enc, prior, inner, outer, w1, wd, wp, bb)


def pairs(target):
    return [(i, target(i)) for i in range(32) if 0 <= target(i) < 32]


SWAP = pairs(lambda i: i ^ 1)
OUTWARD = pairs(lambda i: i - 2 if i % 2 == 0 else i + 2)
INWARD = pairs(lambda i: i + 2 if i % 2 == 0 else i - 2)
LAST = [(i, t) for i, t in INWARD if i % 2 == 1]
ACROSS = pairs(lambda i: i - 1 if i % 2 == 0 else i + 1)


def per_device(
    sections, block_offset, row_base, col_base, fractions, blend,
    conv_first, bias_first, conv_down, bias_down, conv_deep, bias_deep,
):
    def send(value, route):
        return lax.ppermute(value, "rows", route)

    own = sections[0, 0]
    p1 = send(own, OUTWARD)
    p2 = send(own, INWARD)
    a = send(own, SWAP)
    f1 = send(p1, OUTWARD)
    f2 = send(p2, LAST)
    sp1 = send(p1, SWAP)
    sp2 = send(p2, SWAP)
    sf1 = send(f1, SWAP)
    w1, wd, wp, bb = make_weights(
        conv_first, conv_down, conv_deep, bias_first, bias_down, bias_deep
    )
    pay, enc = make_warp(
        block_offset, row_base, col_base, fractions, blend,
        (own, a, p1, sp1, p2, sp2, f1, sf1, f2),
    )
    got = lax.all_to_all(pay, "gz", 0, 0)
    prior = lax.all_to_all(make_prior(got), "gz", 0, 0)
    edges = jnp.stack(
        [
            jnp.concatenate([enc[0:8], enc[120:128]], axis=0),
            jnp.concatenate([prior[0, 0:8], prior[7, 8:16]], axis=0),
        ]
    )
    inner = send(edges, SWAP)
    outer = send(edges, ACROSS)
    return make_encoder(enc, prior, inner, outer, w1, wd, wp, bb)


def solution(mesh):
    return jax.shard_map(
        per_device,
        mesh=mesh,
        in_specs=(
            P(None, "gz", "rows", None),
            P(None, "gz", "rows", None),
            P(None, "gz", "rows", None),
            P(None, "gz", "rows", None),
            P(None, None, "gz", "rows", None),
            P(None, "gz"),
            P(), P(), P(), P(), P(), P(),
        ),
        out_specs=P(None, "gz", None, "rows", None),
        check_vma=False,
    )
```

```python
import jax
import jax.numpy as jnp
from jax import lax
from jax.experimental import pallas as pl
from jax.experimental.pallas import tpu as pltpu
from jax.sharding import PartitionSpec as P

F32 = jnp.float32
BF16 = jnp.bfloat16
VMEM = pltpu.VMEM


def vspec():
    return pl.BlockSpec(memory_space=pltpu.VMEM)


def sspec():
    return pl.BlockSpec(memory_space=pltpu.SMEM)


def aspec():
    return pl.BlockSpec(memory_space=pl.ANY)


def iota(shape, dim):
    return lax.broadcasted_iota(jnp.int32, shape, dim)


def weights_kernel(kf, kd, kp, bf, bd, bp, w1, wd, wp, bb):
    row = iota((32, 256), 0)
    lane = iota((32, 256), 1)

    def place(dr):
        return jnp.where(lane == row + 32 * dr, 1.0, 0.0).astype(BF16)

    spots = [place(dr) for dr in range(3)]

    def base(taps):
        return sum(jnp.dot(taps[dr], spots[dr], preferred_element_type=F32) for dr in range(3))

    diagonal = iota((32, 32), 0) == iota((32, 32), 1)

    def upright(line):
        return jnp.sum(jnp.where(diagonal, line, 0.0), axis=1, keepdims=True)

    within = lane & 31
    quarter = (lane >> 5) & 3
    for phase in range(2):
        acc = jnp.zeros((32, 256), F32)
        for dr in range(3):
            for dx in range(3):
                tap = kf[3 * dr + dx].astype(F32)
                value = jnp.where(lane < 128, upright(tap[0:1, :]), upright(tap[1:2, :]))
                hit = (quarter == dx + phase) & (within == 10 + dr)
                acc = acc + jnp.where(hit, value, 0.0)
        for r in range(16):
            moved = acc if r == 0 else pltpu.roll(acc, r, 1)
            w1[pl.ds(phase * 512 + r * 32, 32), :] = moved.astype(BF16)
    for place_at, dx in enumerate((1, 0, 2)):
        acc = base([kd[3 * dr + dx] for dr in range(3)])
        for r in range(3):
            moved = acc if r == 0 else pltpu.roll(acc, 64 * r, 1)
            wd[pl.ds(place_at * 96 + r * 32, 32), :] = moved.astype(BF16)
    for layer in range(2):
        for dx in range(3):
            acc = base([kp[layer, 3 * dr + dx] for dr in range(3)])
            for r in range(6):
                moved = acc if r == 0 else pltpu.roll(acc, 32 * r, 1)
                wp[layer, pl.ds(dx * 192 + r * 32, 32), :] = moved.astype(BF16)
    for k, line in enumerate((bf[...], bd[...], bp[0:1, :], bp[1:2, :])):
        bb[k] = jnp.broadcast_to(upright(line), (32, 256))


def make_weights(conv_first, conv_down, conv_deep, bias_first, bias_down, bias_deep):
    return pl.pallas_call(
        weights_kernel,
        out_shape=(
            jax.ShapeDtypeStruct((1024, 256), BF16),
            jax.ShapeDtypeStruct((288, 256), BF16),
            jax.ShapeDtypeStruct((2, 576, 256), BF16),
            jax.ShapeDtypeStruct((4, 32, 256), F32),
        ),
        in_specs=[vspec()] * 6,
        out_specs=(vspec(),) * 4,
        cost_estimate=pl.CostEstimate(flops=20_000_000, bytes_accessed=2_000_000, transcendentals=0),
        compiler_params=pltpu.CompilerParams(vmem_limit_bytes=6 << 20),
        name="weights",
    )(conv_first.transpose(0, 2, 1), conv_down, conv_deep, bias_first[None], bias_down[None], bias_deep)


OFFSETS = (0, 1, 2, -1, -2, 3, 4, -3, -4)


def warp_kernel(offs, base, cols, frac, blend, *refs):
    blocks, (pay, enc, S, MJ, MV, sems) = refs[:9], refs[9:]
    core = lax.rem(lax.axis_index("rows"), 2)
    sign = 1 - 2 * core
    copies = []
    for k, off in enumerate(OFFSETS):
        copies.append(pltpu.make_async_copy(blocks[k], S.at[4 + sign * off], sems.at[k]))
    for copy in copies:
        copy.start()
    mats = []
    for j in range(4):
        lo, hi = max(j - 1, 0), min(j + 1, 3)
        wide = (hi - lo + 1) * 128
        src = iota((wide, 128), 0) + (lo - j) * 128
        n = iota((wide, 128), 1)
        if j % 2 == 0:
            x = jnp.where(n < 64, 2 * n, 2 * n - 127)
        else:
            x = jnp.where(n < 64, 2 * n + 1, 2 * n - 128)
        q = frac[1, 0, 0, 0, j].astype(F32) * (1.0 / 256.0)
        target = cols[0, 0, 0, j] + x
        mat = jnp.where(src == target, 1.0 - q, 0.0) + jnp.where(src == target + 1, q, 0.0)
        mats.append(mat.astype(BF16))
    for copy in copies:
        copy.wait()
    for j in range(4):
        lo, hi = max(j - 1, 0), min(j + 1, 3)
        o = offs[0, 0, 0, j]
        for half in range(2):
            window = S[o + 4 + half, :, lo * 128 : (hi + 1) * 128]
            out = jnp.dot(window, mats[j], preferred_element_type=F32)
            MJ[j, half * 128 : (half + 1) * 128, :] = out.astype(BF16).astype(F32)
    lane1 = iota((136, 128), 1)
    for pair in range(2):
        a = MJ[2 * pair, pl.ds(base[0, 0, 0, 2 * pair], 136), :]
        b = MJ[2 * pair + 1, pl.ds(base[0, 0, 0, 2 * pair + 1], 136), :]
        MV[:, pair * 128 : (pair + 1) * 128] = jnp.where(lane1 < 64, a, b)
        MV[:, 256 + pair * 128 : 256 + (pair + 1) * 128] = pltpu.roll(
            jnp.where(lane1 < 64, b, a), 64, 1
        )
    lane = iota((8, 512), 1)
    row = iota((8, 512), 0)
    which = (lane >> 6) & 3
    p = jnp.zeros((8, 512), F32)
    for j in range(4):
        p = jnp.where(which == j, frac[0, 0, 0, 0, j].astype(F32) * (1.0 / 256.0), p)
    rate = jnp.full((8, 512), blend[0, 0], F32)
    top = rate.astype(BF16).astype(F32)
    mid = (rate - top).astype(BF16).astype(F32)
    low = rate - top - mid
    extra = jnp.where(row == 1, p, jnp.where(row == 2, top, jnp.where(row == 3, mid, low)))
    extra = jnp.where(row > 4, 0.0, extra)
    p16 = jnp.concatenate([p, p], axis=0)
    for k in range(8):
        here = MV[16 * k : 16 * k + 16, :]
        below = MV[16 * k + 1 : 16 * k + 17, :]
        enc[16 * k : 16 * k + 16, :] = ((1.0 - p16) * here + p16 * below).astype(BF16)
        pay[k, 0:16, :] = here.astype(BF16)
        tail = MV[16 * k + 16 : 16 * k + 24, :]
        pay[k, 16:24, :] = jnp.where(row == 0, tail, extra).astype(BF16)


def make_warp(offs, base, cols, frac, blend, blocks):
    return pl.pallas_call(
        warp_kernel,
        out_shape=(
            jax.ShapeDtypeStruct((8, 24, 512), BF16),
            jax.ShapeDtypeStruct((128, 512), BF16),
        ),
        in_specs=[sspec()] * 5 + [pl.BlockSpec(memory_space=pltpu.HBM)] + [aspec()] * 8,
        out_specs=(vspec(), vspec()),
        scratch_shapes=[
            VMEM((9, 128, 512), BF16),
            VMEM((4, 264, 128), F32),
            VMEM((136, 512), F32),
            pltpu.SemaphoreType.DMA((9,)),
        ],
        compiler_params=pltpu.CompilerParams(vmem_limit_bytes=8 << 20),
        name="warp",
    )(offs, base, cols, frac, blend, *blocks)


def prior_kernel(got, out, M):
    state = jnp.zeros((16, 512), F32)
    for s in range(8):
        out[s] = state.astype(BF16)
        if s == 7:
            break
        M[s] = got[s].astype(F32)
        p = M[s, 17:18, :]
        rate = M[s, 18:19, :] + M[s, 19:20, :] + M[s, 20:21, :]
        warped = (1.0 - p) * M[s, 0:16, :] + p * M[s, 1:17, :]
        state = rate * state + (1.0 - rate) * warped


def make_prior(got):
    return pl.pallas_call(
        prior_kernel,
        out_shape=jax.ShapeDtypeStruct((8, 16, 512), BF16),
        in_specs=[vspec()],
        out_specs=vspec(),
        scratch_shapes=[VMEM((7, 24, 512), F32)],
        compiler_params=pltpu.CompilerParams(vmem_limit_bytes=4 << 20),
        name="prior",
    )(got)


def encoder_kernel(enc, prior, inner, outer, w1, wd, wp, bb, out, AF, HE, HO, D, T, FS):
    place = lax.axis_index("rows")
    core = lax.rem(place, 2)
    is_top = core == 0
    lane = iota((16, 256), 1)
    zeros8 = jnp.zeros((8, 512), F32)

    def fill(ch, tile, value):
        even, odd = value[:, :256], value[:, 256:]
        rows = pl.ds(16 * tile, 16)
        AF[4 * ch, rows, :] = jnp.where(lane == 0, 0.0, pltpu.roll(odd, 1, 1)).astype(BF16)
        AF[4 * ch + 1, rows, :] = even.astype(BF16)
        AF[4 * ch + 2, rows, :] = odd.astype(BF16)
        AF[4 * ch + 3, rows, :] = jnp.where(lane == 255, 0.0, pltpu.roll(even, 255, 1)).astype(BF16)

    for ch in range(2):
        a = inner[ch].astype(F32)
        b = outer[ch].astype(F32)
        above = jnp.where(is_top, b[8:16], a[8:16])
        below = jnp.where(is_top, a[0:8], b[0:8])
        fill(ch, 0, jnp.concatenate([zeros8, above], axis=0))
        fill(ch, 9, jnp.concatenate([below, zeros8], axis=0))
    for k in range(8):
        fill(0, k + 1, enc[16 * k : 16 * k + 16, :].astype(F32))
        fill(1, k + 1, prior[k].astype(F32))

    def spread(k, n):
        return jnp.concatenate([bb[k]] * n, axis=0)

    bias16 = spread(0, 16)
    for g in range(9):
        data = AF[:, 16 * g : 16 * g + 32, :].reshape(256, 256)
        for phase, H in enumerate((HE, HO)):
            got = jnp.dot(w1[512 * phase : 512 * phase + 512, :], data, preferred_element_type=F32)
            H[512 * g : 512 * g + 512, :] = jnp.maximum(got + bias16, 0.0).astype(BF16)

    @pl.when(place == 0)
    def _():
        HE[0:160, :] = jnp.zeros((160, 256), BF16)
        HO[0:160, :] = jnp.zeros((160, 256), BF16)

    @pl.when(place == 31)
    def _():
        HE[4256:4608, :] = jnp.zeros((352, 256), BF16)
        HO[4256:4608, :] = jnp.zeros((352, 256), BF16)

    def right(v):
        at = iota(v.shape, 1)
        return jnp.where(at == 0, 0.0, pltpu.roll(v, 1, 1))

    def left(v):
        at = iota(v.shape, 1)
        return jnp.where(at == 255, 0.0, pltpu.roll(v, 255, 1))

    bias3 = spread(1, 3)
    for g in range(23):
        even = jnp.dot(wd[0:96, 0:224], HE[192 * g : 192 * g + 224, :], preferred_element_type=F32)
        odd = jnp.dot(wd[96:288, 0:224], HO[192 * g : 192 * g + 224, :], preferred_element_type=F32)
        total = even + right(odd[0:96]) + odd[96:192] + bias3
        D[96 * g : 96 * g + 96, :] = jnp.maximum(total, 0.0).astype(BF16)

    @pl.when(place == 0)
    def _():
        D[0:64, :] = jnp.zeros((64, 256), BF16)

    @pl.when(place == 31)
    def _():
        D[2112:2208, :] = jnp.zeros((96, 256), BF16)

    bias6 = spread(2, 6)
    for g in range(11):
        got = jnp.dot(wp[0], D[192 * g : 192 * g + 256, :], preferred_element_type=F32)
        total = got[192:384] + right(got[0:192]) + left(got[384:576]) + bias6
        T[192 * g : 192 * g + 192, :] = jnp.maximum(total, 0.0).astype(BF16)
    T[2112:2176, :] = jnp.zeros((64, 256), BF16)

    @pl.when(place == 0)
    def _():
        T[0:32, :] = jnp.zeros((32, 256), BF16)

    @pl.when(place == 31)
    def _():
        T[2080:2112, :] = jnp.zeros((32, 256), BF16)

    bias7 = spread(3, 6)
    for g in range(11):
        got = jnp.dot(wp[1], T[192 * g : 192 * g + 256, :], preferred_element_type=F32)
        total = got[192:384] + right(got[0:192]) + left(got[384:576]) + bias7
        for r in range(6):
            for part in range(4):
                for half in range(2):
                    FS[half, part, 48 * g + 8 * r : 48 * g + 8 * r + 8, :] = total[
                        32 * r + 8 * part : 32 * r + 8 * part + 8, 128 * half : 128 * half + 128
                    ]
    for ch in range(32):
        for half in range(2):
            out[0, 0, ch, :, 128 * half : 128 * half + 128] = FS[
                half, ch // 8, pl.ds(ch % 8, 64, stride=8), :
            ].astype(BF16)


def make_encoder(enc, prior, inner, outer, w1, wd, wp, bb):
    return pl.pallas_call(
        encoder_kernel,
        out_shape=jax.ShapeDtypeStruct((1, 1, 32, 64, 256), BF16),
        in_specs=[vspec()] * 8,
        out_specs=vspec(),
        scratch_shapes=[
            VMEM((8, 160, 256), BF16),
            VMEM((4608, 256), BF16),
            VMEM((4608, 256), BF16),
            VMEM((2208, 256), BF16),
            VMEM((2176, 256), BF16),
            VMEM((2, 4, 528, 128), F32),
        ],
        compiler_params=pltpu.CompilerParams(vmem_limit_bytes=20 << 20),
        name="encoder",
    )(enc, prior, inner, outer, w1, wd, wp, bb)


def pairs(target):
    return [(i, target(i)) for i in range(32) if 0 <= target(i) < 32]


SWAP = pairs(lambda i: i ^ 1)
OUTWARD = pairs(lambda i: i - 2 if i % 2 == 0 else i + 2)
INWARD = pairs(lambda i: i + 2 if i % 2 == 0 else i - 2)
LAST = [(i, t) for i, t in INWARD if i % 2 == 1]
ACROSS = pairs(lambda i: i - 1 if i % 2 == 0 else i + 1)


def per_device(
    sections, block_offset, row_base, col_base, fractions, blend,
    conv_first, bias_first, conv_down, bias_down, conv_deep, bias_deep,
):
    def send(value, route):
        return lax.ppermute(value, "rows", route)

    own = sections[0, 0]
    p1 = send(own, OUTWARD)
    p2 = send(own, INWARD)
    a = send(own, SWAP)
    f1 = send(p1, OUTWARD)
    f2 = send(p2, LAST)
    sp1 = send(p1, SWAP)
    sp2 = send(p2, SWAP)
    sf1 = send(f1, SWAP)
    w1, wd, wp, bb = make_weights(
        conv_first, conv_down, conv_deep, bias_first, bias_down, bias_deep
    )
    pay, enc = make_warp(
        block_offset, row_base, col_base, fractions, blend,
        (own, a, p1, sp1, p2, sp2, f1, sf1, f2),
    )
    got = lax.all_to_all(pay, "gz", 0, 0)
    given = make_prior(got)
    prior = lax.all_to_all(given, "gz", 0, 0)
    edges = jnp.stack(
        [
            jnp.concatenate([enc[0:8], enc[120:128]], axis=0),
            jnp.concatenate([prior[0, 0:8], prior[7, 8:16]], axis=0),
        ]
    )
    inner = send(edges, SWAP)
    outer = send(edges, ACROSS)
    return make_encoder(enc, prior, inner, outer, w1, wd, wp, bb)


def solution(mesh):
    return jax.shard_map(
        per_device,
        mesh=mesh,
        in_specs=(
            P(None, "gz", "rows", None),
            P(None, "gz", "rows", None),
            P(None, "gz", "rows", None),
            P(None, "gz", "rows", None),
            P(None, None, "gz", "rows", None),
            P(None, "gz"),
            P(), P(), P(), P(), P(), P(),
        ),
        out_specs=P(None, "gz", None, "rows", None),
        check_vma=False,
    )
```

```python
import jax
import jax.numpy as jnp
from jax import lax
from jax.experimental import pallas as pl
from jax.experimental.pallas import tpu as pltpu
from jax.sharding import PartitionSpec as P

F32 = jnp.float32
BF16 = jnp.bfloat16
VMEM = pltpu.VMEM


def vspec():
    return pl.BlockSpec(memory_space=pltpu.VMEM)


def sspec():
    return pl.BlockSpec(memory_space=pltpu.SMEM)


def iota(shape, dim):
    return lax.broadcasted_iota(jnp.int32, shape, dim)


def weights_kernel(kf, kd, kp, bf, bd, bp, w1, wd, wp, bb):
    row = iota((32, 256), 0)
    lane = iota((32, 256), 1)

    def place(dr):
        return jnp.where(lane == row + 32 * dr, 1.0, 0.0).astype(BF16)

    spots = [place(dr) for dr in range(3)]

    def base(taps):
        return sum(jnp.dot(taps[dr], spots[dr], preferred_element_type=F32) for dr in range(3))

    diagonal = iota((32, 32), 0) == iota((32, 32), 1)

    def upright(line):
        return jnp.sum(jnp.where(diagonal, line, 0.0), axis=1, keepdims=True)

    within = lane & 31
    quarter = (lane >> 5) & 3
    for phase in range(2):
        acc = jnp.zeros((32, 256), F32)
        for dr in range(3):
            for dx in range(3):
                tap = kf[3 * dr + dx].astype(F32)
                value = jnp.where(lane < 128, upright(tap[0:1, :]), upright(tap[1:2, :]))
                hit = (quarter == dx + phase) & (within == 10 + dr)
                acc = acc + jnp.where(hit, value, 0.0)
        for r in range(16):
            moved = acc if r == 0 else pltpu.roll(acc, r, 1)
            w1[pl.ds(phase * 512 + r * 32, 32), :] = moved.astype(BF16)
    for place_at, dx in enumerate((1, 0, 2)):
        acc = base([kd[3 * dr + dx] for dr in range(3)])
        for r in range(3):
            moved = acc if r == 0 else pltpu.roll(acc, 64 * r, 1)
            wd[pl.ds(place_at * 96 + r * 32, 32), :] = moved.astype(BF16)
    for layer in range(2):
        for dx in range(3):
            acc = base([kp[layer, 3 * dr + dx] for dr in range(3)])
            for r in range(6):
                moved = acc if r == 0 else pltpu.roll(acc, 32 * r, 1)
                wp[layer, pl.ds(dx * 192 + r * 32, 32), :] = moved.astype(BF16)
    for k, line in enumerate((bf[...], bd[...], bp[0:1, :], bp[1:2, :])):
        bb[k] = jnp.broadcast_to(upright(line), (32, 256))


def make_weights(conv_first, conv_down, conv_deep, bias_first, bias_down, bias_deep):
    return pl.pallas_call(
        weights_kernel,
        out_shape=(
            jax.ShapeDtypeStruct((1024, 256), BF16),
            jax.ShapeDtypeStruct((288, 256), BF16),
            jax.ShapeDtypeStruct((2, 576, 256), BF16),
            jax.ShapeDtypeStruct((4, 32, 256), F32),
        ),
        in_specs=[vspec()] * 6,
        out_specs=(vspec(),) * 4,
        cost_estimate=pl.CostEstimate(flops=20_000_000, bytes_accessed=2_000_000, transcendentals=0),
        compiler_params=pltpu.CompilerParams(vmem_limit_bytes=6 << 20),
        name="weights",
    )(conv_first.transpose(0, 2, 1), conv_down, conv_deep, bias_first[None], bias_down[None], bias_deep)


OFFSETS = (0, 1, 2, -1, -2, 3, 4, -3, -4)


def warp_kernel(offs, base, cols, frac, blend, *refs):
    blocks, (pay, enc, OWN, MJ, MV, sem) = refs[:9], refs[9:]
    core = lax.rem(lax.axis_index("rows"), 2)
    sign = 1 - 2 * core
    fetch = pltpu.make_async_copy(blocks[0], OWN, sem)
    fetch.start()
    mats = []
    for j in range(4):
        lo, hi = max(j - 1, 0), min(j + 1, 3)
        wide = (hi - lo + 1) * 128
        src = iota((wide, 128), 0) + (lo - j) * 128
        n = iota((wide, 128), 1)
        if j % 2 == 0:
            x = jnp.where(n < 64, 2 * n, 2 * n - 127)
        else:
            x = jnp.where(n < 64, 2 * n + 1, 2 * n - 128)
        q = frac[1, 0, 0, 0, j].astype(F32) * (1.0 / 256.0)
        target = cols[0, 0, 0, j] + x
        mat = jnp.where(src == target, 1.0 - q, 0.0) + jnp.where(src == target + 1, q, 0.0)
        mats.append(mat.astype(BF16))
    fetch.wait()
    by_offset = dict(zip(OFFSETS, (OWN,) + tuple(blocks[1:])))
    for j in range(4):
        lo, hi = max(j - 1, 0), min(j + 1, 3)
        o = offs[0, 0, 0, j]
        for half in range(2):

            def take(ref, j=j, lo=lo, hi=hi, half=half):
                out = jnp.dot(ref[:, lo * 128 : (hi + 1) * 128], mats[j], preferred_element_type=F32)
                MJ[j, half * 128 : (half + 1) * 128, :] = out.astype(BF16).astype(F32)

            wanted = sign * (o + half)
            for off in range(-4, 5):
                pl.when(wanted == off)(lambda off=off: take(by_offset[off]))
    lane1 = iota((136, 128), 1)
    for pair in range(2):
        a = MJ[2 * pair, pl.ds(base[0, 0, 0, 2 * pair], 136), :]
        b = MJ[2 * pair + 1, pl.ds(base[0, 0, 0, 2 * pair + 1], 136), :]
        MV[:, pair * 128 : (pair + 1) * 128] = jnp.where(lane1 < 64, a, b)
        MV[:, 256 + pair * 128 : 256 + (pair + 1) * 128] = pltpu.roll(
            jnp.where(lane1 < 64, b, a), 64, 1
        )
    lane = iota((8, 512), 1)
    row = iota((8, 512), 0)
    which = (lane >> 6) & 3
    p = jnp.zeros((8, 512), F32)
    for j in range(4):
        p = jnp.where(which == j, frac[0, 0, 0, 0, j].astype(F32) * (1.0 / 256.0), p)
    rate = jnp.full((8, 512), blend[0, 0], F32)
    top = rate.astype(BF16).astype(F32)
    mid = (rate - top).astype(BF16).astype(F32)
    low = rate - top - mid
    extra = jnp.where(row == 1, p, jnp.where(row == 2, top, jnp.where(row == 3, mid, low)))
    extra = jnp.where(row > 4, 0.0, extra)
    p16 = jnp.concatenate([p, p], axis=0)
    for k in range(8):
        here = MV[16 * k : 16 * k + 16, :]
        below = MV[16 * k + 1 : 16 * k + 17, :]
        enc[16 * k : 16 * k + 16, :] = ((1.0 - p16) * here + p16 * below).astype(BF16)
        pay[k, 0:16, :] = here.astype(BF16)
        tail = MV[16 * k + 16 : 16 * k + 24, :]
        pay[k, 16:24, :] = jnp.where(row == 0, tail, extra).astype(BF16)


def make_warp(offs, base, cols, frac, blend, blocks):
    own = pltpu.with_memory_space_constraint(blocks[0], pltpu.HBM)
    return pl.pallas_call(
        warp_kernel,
        out_shape=(
            jax.ShapeDtypeStruct((8, 24, 512), BF16),
            jax.ShapeDtypeStruct((128, 512), BF16),
        ),
        in_specs=[sspec()] * 5 + [pl.BlockSpec(memory_space=pltpu.HBM)] + [vspec()] * 8,
        out_specs=(vspec(), vspec()),
        scratch_shapes=[
            VMEM((128, 512), BF16),
            VMEM((4, 264, 128), F32),
            VMEM((136, 512), F32),
            pltpu.SemaphoreType.DMA,
        ],
        compiler_params=pltpu.CompilerParams(vmem_limit_bytes=8 << 20),
        name="warp",
    )(offs, base, cols, frac, blend, own, *blocks[1:])


def prior_kernel(got, out, M):
    state = jnp.zeros((16, 512), F32)
    for s in range(8):
        out[s] = state.astype(BF16)
        if s == 7:
            break
        M[s] = got[s].astype(F32)
        p = M[s, 17:18, :]
        rate = M[s, 18:19, :] + M[s, 19:20, :] + M[s, 20:21, :]
        warped = (1.0 - p) * M[s, 0:16, :] + p * M[s, 1:17, :]
        state = rate * state + (1.0 - rate) * warped


def make_prior(got):
    return pl.pallas_call(
        prior_kernel,
        out_shape=jax.ShapeDtypeStruct((8, 16, 512), BF16),
        in_specs=[vspec()],
        out_specs=vspec(),
        scratch_shapes=[VMEM((7, 24, 512), F32)],
        compiler_params=pltpu.CompilerParams(vmem_limit_bytes=4 << 20),
        name="prior",
    )(got)


def right(v):
    at = iota(v.shape, 1)
    return jnp.where(at == 0, 0.0, pltpu.roll(v, 1, 1))


def left(v):
    at = iota(v.shape, 1)
    return jnp.where(at == 255, 0.0, pltpu.roll(v, 255, 1))


def fill(AF, ch, tile, value):
    even, odd = value[:, :256], value[:, 256:]
    rows = pl.ds(16 * tile, 16)
    AF[4 * ch, rows, :] = right(odd).astype(BF16)
    AF[4 * ch + 1, rows, :] = even.astype(BF16)
    AF[4 * ch + 2, rows, :] = odd.astype(BF16)
    AF[4 * ch + 3, rows, :] = left(even).astype(BF16)


def spread(bb, k, n):
    return jnp.concatenate([bb[k]] * n, axis=0)


def first_layer(AF, at, w1, bias, HE, HO, to):
    data = AF[:, at : at + 32, :].reshape(256, 256)
    for phase, H in enumerate((HE, HO)):
        got = jnp.dot(w1[512 * phase : 512 * phase + 512, :], data, preferred_element_type=F32)
        H[32 * to : 32 * to + 512, :] = jnp.maximum(got + bias, 0.0).astype(BF16)


def down_layer(HE, HO, at, wd, bias, D, to):
    even = jnp.dot(wd[0:96, 0:224], HE[32 * at : 32 * at + 224, :], preferred_element_type=F32)
    odd = jnp.dot(wd[96:288, 0:224], HO[32 * at : 32 * at + 224, :], preferred_element_type=F32)
    total = even + right(odd[0:96]) + odd[96:192] + bias
    D[32 * to : 32 * to + 96, :] = jnp.maximum(total, 0.0).astype(BF16)


def deep_sum(F, at, w, bias):
    got = jnp.dot(w[...], F[32 * at : 32 * at + 256, :], preferred_element_type=F32)
    return got[192:384] + right(got[0:192]) + left(got[384:576]) + bias


def deep_layer(D, at, w, bias, T, to):
    T[32 * to : 32 * to + 192, :] = jnp.maximum(deep_sum(D, at, w, bias), 0.0).astype(BF16)


def last_layer(T, at, w, bias, FS, to):
    total = deep_sum(T, at, w, bias)
    for r in range(6):
        for part in range(4):
            for half in range(2):
                FS[half, part, 8 * (to + r) : 8 * (to + r) + 8, :] = total[
                    32 * r + 8 * part : 32 * r + 8 * part + 8, 128 * half : 128 * half + 128
                ]


def gather_rows(FS, start, count, O):
    for ch in range(32):
        for half in range(2):
            O[ch, :, 128 * half : 128 * half + 128] = FS[
                half, ch // 8, pl.ds(8 * start + ch % 8, count, stride=8), :
            ].astype(BF16)


def inner_kernel(enc, prior, w1, wd, wp, bb, out, keep_h, keep_d, keep_t, AF, HE, HO, D, T, FS, O, sem):
    for k in range(8):
        fill(AF, 0, k, enc[16 * k : 16 * k + 16, :].astype(F32))
        fill(AF, 1, k, prior[k].astype(F32))
    bias = spread(bb, 0, 16)
    for g in range(7):
        first_layer(AF, 16 * g, w1, bias, HE, HO, 16 * g)
    for phase, H in enumerate((HE, HO)):
        keep_h[phase, 0] = H[0:128, :]
        keep_h[phase, 1] = H[3456:3584, :]
    bias = spread(bb, 1, 3)
    for g in range(18):
        down_layer(HE, HO, 6 * g + 2, wd, bias, D, 3 * g)
    keep_d[0] = D[0:256, :]
    keep_d[1] = D[1472:1728, :]
    bias = spread(bb, 2, 6)
    for g in range(8):
        deep_layer(D, 6 * g + 3, wp.at[0], bias, T, 6 * g)
    keep_t[0] = T[0:384, :]
    keep_t[1] = T[1152:1536, :]
    bias = spread(bb, 3, 6)
    for g in range(6):
        last_layer(T, 6 * g, wp.at[1], bias, FS, 6 * g)
    gather_rows(FS, 4, 32, O)
    copy = pltpu.make_async_copy(O, out.at[0, 0, :, pl.ds(16, 32), :], sem)
    copy.start()
    copy.wait()


def make_inner(enc, prior, w1, wd, wp, bb):
    return pl.pallas_call(
        inner_kernel,
        out_shape=(
            jax.ShapeDtypeStruct((1, 1, 32, 64, 256), BF16),
            jax.ShapeDtypeStruct((2, 2, 128, 256), BF16),
            jax.ShapeDtypeStruct((2, 256, 256), BF16),
            jax.ShapeDtypeStruct((2, 384, 256), BF16),
        ),
        in_specs=[vspec()] * 6,
        out_specs=(pl.BlockSpec(memory_space=pltpu.HBM), vspec(), vspec(), vspec()),
        scratch_shapes=[
            VMEM((8, 128, 256), BF16),
            VMEM((3584, 256), BF16),
            VMEM((3584, 256), BF16),
            VMEM((1728, 256), BF16),
            VMEM((1536, 256), BF16),
            VMEM((2, 4, 288, 128), F32),
            VMEM((32, 32, 256), BF16),
            pltpu.SemaphoreType.DMA,
        ],
        compiler_params=pltpu.CompilerParams(vmem_limit_bytes=16 << 20),
        cost_estimate=pl.CostEstimate(
            flops=6_000_000_000, bytes_accessed=4_000_000, transcendentals=0
        ),
        name="middle",
    )(enc, prior, w1, wd, wp, bb)


def outer_kernel(
    enc, prior, inner, outer, w1, wd, wp, bb, keep_h, keep_d, keep_t, got, out,
    AF, HE, HO, D, T, FS, O, sems,
):
    place = lax.axis_index("rows")
    is_top = lax.rem(place, 2) == 0
    zeros8 = jnp.zeros((8, 512), F32)
    for ch in range(2):
        a = inner[ch].astype(F32)
        b = outer[ch].astype(F32)
        above = jnp.where(is_top, b[8:16], a[8:16])
        below = jnp.where(is_top, a[0:8], b[0:8])
        fill(AF.at[0], ch, 0, jnp.concatenate([zeros8, above], axis=0))
        fill(AF.at[1], ch, 1, jnp.concatenate([below, zeros8], axis=0))
    fill(AF.at[0], 0, 1, enc[0:16, :].astype(F32))
    fill(AF.at[0], 1, 1, prior[0].astype(F32))
    fill(AF.at[1], 0, 0, enc[112:128, :].astype(F32))
    fill(AF.at[1], 1, 0, prior[7].astype(F32))
    bias = spread(bb, 0, 16)
    for phase, H in enumerate((HE, HO)):
        H[0, 512:640, :] = keep_h[phase, 0]
        H[1, 0:128, :] = keep_h[phase, 1]
    first_layer(AF.at[0], 0, w1, bias, HE.at[0], HO.at[0], 0)
    first_layer(AF.at[1], 0, w1, bias, HE.at[1], HO.at[1], 4)

    @pl.when(place == 0)
    def _():
        HE[0, 0:160, :] = jnp.zeros((160, 256), BF16)
        HO[0, 0:160, :] = jnp.zeros((160, 256), BF16)

    @pl.when(place == 31)
    def _():
        HE[1, 288:640, :] = jnp.zeros((352, 256), BF16)
        HO[1, 288:640, :] = jnp.zeros((352, 256), BF16)

    bias = spread(bb, 1, 3)
    D[0, 288:544, :] = keep_d[0]
    D[1, 0:256, :] = keep_d[1]
    for g in range(3):
        down_layer(HE.at[0], HO.at[0], 6 * g, wd, bias, D.at[0], 3 * g)
    for g in range(2):
        down_layer(HE.at[1], HO.at[1], 6 * g + 2, wd, bias, D.at[1], 3 * g + 8)

    @pl.when(place == 0)
    def _():
        D[0, 0:64, :] = jnp.zeros((64, 256), BF16)

    @pl.when(place == 31)
    def _():
        D[1, 352:448, :] = jnp.zeros((96, 256), BF16)

    bias = spread(bb, 2, 6)
    T[0, 384:768, :] = keep_t[0]
    T[1, 0:384, :] = keep_t[1]
    for g in range(2):
        deep_layer(D.at[0], 6 * g, wp.at[0], bias, T.at[0], 6 * g)
    deep_layer(D.at[1], 5, wp.at[0], bias, T.at[1], 12)
    T[1, 576:768, :] = jnp.zeros((192, 256), BF16)

    @pl.when(place == 0)
    def _():
        T[0, 0:32, :] = jnp.zeros((32, 256), BF16)

    @pl.when(place == 31)
    def _():
        T[1, 544:576, :] = jnp.zeros((32, 256), BF16)

    bias = spread(bb, 3, 6)
    copies = []
    for side in range(2):
        for g in range(3):
            last_layer(T.at[side], 6 * g, wp.at[1], bias, FS.at[side], 6 * g)
        gather_rows(FS.at[side], 0, 16, O.at[side])
        copy = pltpu.make_async_copy(
            O.at[side], out.at[0, 0, :, pl.ds(48 * side, 16), :], sems.at[side]
        )
        copy.start()
        copies.append(copy)
    for copy in copies:
        copy.wait()


def make_outer(enc, prior, inner, outer, w1, wd, wp, bb, keep_h, keep_d, keep_t, got):
    hbm = pl.BlockSpec(memory_space=pltpu.HBM)
    return pl.pallas_call(
        outer_kernel,
        out_shape=jax.ShapeDtypeStruct((1, 1, 32, 64, 256), BF16),
        in_specs=[vspec()] * 11 + [hbm],
        out_specs=hbm,
        scratch_shapes=[
            VMEM((2, 8, 32, 256), BF16),
            VMEM((2, 640, 256), BF16),
            VMEM((2, 640, 256), BF16),
            VMEM((2, 544, 256), BF16),
            VMEM((2, 768, 256), BF16),
            VMEM((2, 2, 4, 144, 128), F32),
            VMEM((2, 32, 16, 256), BF16),
            pltpu.SemaphoreType.DMA((2,)),
        ],
        input_output_aliases={11: 0},
        compiler_params=pltpu.CompilerParams(vmem_limit_bytes=16 << 20),
        name="border",
    )(enc, prior, inner, outer, w1, wd, wp, bb, keep_h, keep_d, keep_t, got)


def pairs(target):
    return [(i, target(i)) for i in range(32) if 0 <= target(i) < 32]


SWAP = pairs(lambda i: i ^ 1)
OUTWARD = pairs(lambda i: i - 2 if i % 2 == 0 else i + 2)
INWARD = pairs(lambda i: i + 2 if i % 2 == 0 else i - 2)
LAST = [(i, t) for i, t in INWARD if i % 2 == 1]
ACROSS = pairs(lambda i: i - 1 if i % 2 == 0 else i + 1)


def per_device(
    sections, block_offset, row_base, col_base, fractions, blend,
    conv_first, bias_first, conv_down, bias_down, conv_deep, bias_deep,
):
    def send(value, route):
        return lax.ppermute(value, "rows", route)

    own = sections[0, 0]
    p1 = send(own, OUTWARD)
    p2 = send(own, INWARD)
    a = send(own, SWAP)
    f1 = send(p1, OUTWARD)
    f2 = send(p2, LAST)
    sp1 = send(p1, SWAP)
    sp2 = send(p2, SWAP)
    sf1 = send(f1, SWAP)
    w1, wd, wp, bb = make_weights(
        conv_first, conv_down, conv_deep, bias_first, bias_down, bias_deep
    )
    pay, enc = make_warp(
        block_offset, row_base, col_base, fractions, blend,
        (own, a, p1, sp1, p2, sp2, f1, sf1, f2),
    )
    got = lax.all_to_all(pay, "gz", 0, 0)
    given = make_prior(got)
    prior = lax.all_to_all(given, "gz", 0, 0)
    edges = jnp.stack(
        [
            jnp.concatenate([enc[0:8], enc[120:128]], axis=0),
            jnp.concatenate([prior[0, 0:8], prior[7, 8:16]], axis=0),
        ]
    )
    inner = send(edges, SWAP)
    outer = send(edges, ACROSS)
    got, keep_h, keep_d, keep_t = make_inner(enc, prior, w1, wd, wp, bb)
    return make_outer(
        enc, prior, inner, outer, w1, wd, wp, bb, keep_h, keep_d, keep_t, got
    )


def solution(mesh):
    return jax.shard_map(
        per_device,
        mesh=mesh,
        in_specs=(
            P(None, "gz", "rows", None),
            P(None, "gz", "rows", None),
            P(None, "gz", "rows", None),
            P(None, "gz", "rows", None),
            P(None, None, "gz", "rows", None),
            P(None, "gz"),
            P(), P(), P(), P(), P(), P(),
        ),
        out_specs=P(None, "gz", None, "rows", None),
        check_vma=False,
    )
```

```python
import jax
import jax.numpy as jnp
from jax import lax
from jax.experimental import pallas as pl
from jax.experimental.pallas import tpu as pltpu
from jax.sharding import PartitionSpec as P

F32 = jnp.float32
BF16 = jnp.bfloat16
VMEM = pltpu.VMEM


def vspec():
    return pl.BlockSpec(memory_space=pltpu.VMEM)


def sspec():
    return pl.BlockSpec(memory_space=pltpu.SMEM)


def iota(shape, dim):
    return lax.broadcasted_iota(jnp.int32, shape, dim)


def weights_kernel(kf, kd, kp, bf, bd, bp, w1, wd, wp, bb):
    row = iota((32, 256), 0)
    lane = iota((32, 256), 1)

    def place(dr):
        return jnp.where(lane == row + 32 * dr, 1.0, 0.0).astype(BF16)

    spots = [place(dr) for dr in range(3)]

    def base(taps):
        return sum(jnp.dot(taps[dr], spots[dr], preferred_element_type=F32) for dr in range(3))

    diagonal = iota((32, 32), 0) == iota((32, 32), 1)

    def upright(line):
        return jnp.sum(jnp.where(diagonal, line, 0.0), axis=1, keepdims=True)

    within = lane & 31
    quarter = (lane >> 5) & 3
    for phase in range(2):
        acc = jnp.zeros((32, 256), F32)
        for dr in range(3):
            for dx in range(3):
                tap = kf[3 * dr + dx].astype(F32)
                value = jnp.where(lane < 128, upright(tap[0:1, :]), upright(tap[1:2, :]))
                hit = (quarter == dx + phase) & (within == 10 + dr)
                acc = acc + jnp.where(hit, value, 0.0)
        for r in range(16):
            moved = acc if r == 0 else pltpu.roll(acc, r, 1)
            w1[pl.ds(phase * 512 + r * 32, 32), :] = moved.astype(BF16)
    for place_at, dx in enumerate((1, 0, 2)):
        acc = base([kd[3 * dr + dx] for dr in range(3)])
        for r in range(3):
            moved = acc if r == 0 else pltpu.roll(acc, 64 * r, 1)
            wd[pl.ds(place_at * 96 + r * 32, 32), :] = moved.astype(BF16)
    for layer in range(2):
        for dx in range(3):
            acc = base([kp[layer, 3 * dr + dx] for dr in range(3)])
            for r in range(6):
                moved = acc if r == 0 else pltpu.roll(acc, 32 * r, 1)
                wp[layer, pl.ds(dx * 192 + r * 32, 32), :] = moved.astype(BF16)
    for k, line in enumerate((bf[...], bd[...], bp[0:1, :], bp[1:2, :])):
        bb[k] = jnp.broadcast_to(upright(line), (32, 256))


def make_weights(conv_first, conv_down, conv_deep, bias_first, bias_down, bias_deep):
    return pl.pallas_call(
        weights_kernel,
        out_shape=(
            jax.ShapeDtypeStruct((1024, 256), BF16),
            jax.ShapeDtypeStruct((288, 256), BF16),
            jax.ShapeDtypeStruct((2, 576, 256), BF16),
            jax.ShapeDtypeStruct((4, 32, 256), F32),
        ),
        in_specs=[vspec()] * 6,
        out_specs=(vspec(),) * 4,
        cost_estimate=pl.CostEstimate(flops=20_000_000, bytes_accessed=2_000_000, transcendentals=0),
        compiler_params=pltpu.CompilerParams(vmem_limit_bytes=6 << 20),
        name="weights",
    )(conv_first.transpose(0, 2, 1), conv_down, conv_deep, bias_first[None], bias_down[None], bias_deep)


OFFSETS = (0, 1, 2, -1, -2, 3, 4, -3, -4)


def warp_kernel(offs, base, cols, frac, blend, *refs):
    blocks, (pay, enc, S, MJ, MV, sem) = refs[:9], refs[9:]
    core = lax.rem(lax.axis_index("rows"), 2)
    sign = 1 - 2 * core
    fetch = pltpu.make_async_copy(blocks[0], S.at[4], sem)
    fetch.start()
    for k, off in enumerate(OFFSETS):
        if k > 0:
            S[4 + sign * off] = blocks[k][...]
    mats = []
    for j in range(4):
        lo, hi = max(j - 1, 0), min(j + 1, 3)
        wide = (hi - lo + 1) * 128
        src = iota((wide, 128), 0) + (lo - j) * 128
        n = iota((wide, 128), 1)
        if j % 2 == 0:
            x = jnp.where(n < 64, 2 * n, 2 * n - 127)
        else:
            x = jnp.where(n < 64, 2 * n + 1, 2 * n - 128)
        q = frac[1, 0, 0, 0, j].astype(F32) * (1.0 / 256.0)
        target = cols[0, 0, 0, j] + x
        mat = jnp.where(src == target, 1.0 - q, 0.0) + jnp.where(src == target + 1, q, 0.0)
        mats.append(mat.astype(BF16))
    fetch.wait()
    for j in range(4):
        lo, hi = max(j - 1, 0), min(j + 1, 3)
        first = offs[0, 0, 0, j] + 4
        window = S[pl.ds(first, 2), :, lo * 128 : (hi + 1) * 128].reshape(256, (hi - lo + 1) * 128)
        out = jnp.dot(window, mats[j], preferred_element_type=F32)
        MJ[j, 0:256, :] = out.astype(BF16).astype(F32)
    lane1 = iota((136, 128), 1)
    for pair in range(2):
        a = MJ[2 * pair, pl.ds(base[0, 0, 0, 2 * pair], 136), :]
        b = MJ[2 * pair + 1, pl.ds(base[0, 0, 0, 2 * pair + 1], 136), :]
        MV[:, pair * 128 : (pair + 1) * 128] = jnp.where(lane1 < 64, a, b)
        MV[:, 256 + pair * 128 : 256 + (pair + 1) * 128] = pltpu.roll(
            jnp.where(lane1 < 64, b, a), 64, 1
        )
    lane = iota((8, 512), 1)
    which = (lane >> 6) & 3
    p = jnp.zeros((8, 512), F32)
    for j in range(4):
        p = jnp.where(which == j, frac[0, 0, 0, 0, j].astype(F32) * (1.0 / 256.0), p)
    rate = jnp.full((16, 128), blend[0, 0], F32)
    top = rate.astype(BF16).astype(F32)
    mid = (rate - top).astype(BF16).astype(F32)
    low = rate - top - mid
    row = iota((16, 128), 0)
    extra = jnp.where(row == 8, top, jnp.where(row == 9, mid, jnp.where(row == 10, low, 0.0)))
    for c in range(4):
        extra = jnp.where(row == 4 + c, p[0:1, 128 * c : 128 * c + 128], extra)
    p16 = jnp.concatenate([p, p], axis=0)
    for k in range(8):
        here = MV[16 * k : 16 * k + 16, :]
        below = MV[16 * k + 1 : 16 * k + 17, :]
        enc[16 * k : 16 * k + 16, :] = ((1.0 - p16) * here + p16 * below).astype(BF16)
        pay[k, :, 0:512] = here.astype(BF16)
        tail = extra
        for c in range(4):
            piece = MV[16 * k + 16 : 16 * k + 17, 128 * c : 128 * c + 128]
            tail = jnp.where(row == c, piece, tail)
        pay[k, :, 512:640] = tail.astype(BF16)


def make_warp(offs, base, cols, frac, blend, blocks):
    own = pltpu.with_memory_space_constraint(blocks[0], pltpu.HBM)
    return pl.pallas_call(
        warp_kernel,
        out_shape=(
            jax.ShapeDtypeStruct((8, 16, 640), BF16),
            jax.ShapeDtypeStruct((128, 512), BF16),
        ),
        in_specs=[sspec()] * 5 + [pl.BlockSpec(memory_space=pltpu.HBM)] + [vspec()] * 8,
        out_specs=(vspec(), vspec()),
        scratch_shapes=[
            VMEM((9, 128, 512), BF16),
            VMEM((4, 264, 128), F32),
            VMEM((136, 512), F32),
            pltpu.SemaphoreType.DMA,
        ],
        compiler_params=pltpu.CompilerParams(vmem_limit_bytes=8 << 20),
        name="warp",
    )(offs, base, cols, frac, blend, own, *blocks[1:])


def prior_kernel(got, out, M):
    state = jnp.zeros((16, 512), F32)
    for s in range(8):
        out[s] = state.astype(BF16)
        if s == 7:
            break
        M[s, 0:16, :] = got[s, :, 0:512].astype(F32)
        extra = got[s, :, 512:640].astype(F32)
        for c in range(4):
            M[s, 16:17, 128 * c : 128 * c + 128] = extra[c : c + 1, :]
        p = jnp.concatenate([extra[4 + c : 5 + c, :] for c in range(4)], axis=1)
        rate = extra[8:9, 0:1] + extra[9:10, 0:1] + extra[10:11, 0:1]
        warped = (1.0 - p) * M[s, 0:16, :] + p * M[s, 1:17, :]
        state = rate * state + (1.0 - rate) * warped


def make_prior(got):
    return pl.pallas_call(
        prior_kernel,
        out_shape=jax.ShapeDtypeStruct((8, 16, 512), BF16),
        in_specs=[vspec()],
        out_specs=vspec(),
        scratch_shapes=[VMEM((7, 24, 512), F32)],
        compiler_params=pltpu.CompilerParams(vmem_limit_bytes=4 << 20),
        name="prior",
    )(got)


def right(v):
    at = iota(v.shape, 1)
    return jnp.where(at == 0, 0.0, pltpu.roll(v, 1, 1))


def left(v):
    at = iota(v.shape, 1)
    return jnp.where(at == 255, 0.0, pltpu.roll(v, 255, 1))


def fill(AF, ch, tile, value):
    even, odd = value[:, :256], value[:, 256:]
    rows = pl.ds(16 * tile, 16)
    AF[4 * ch, rows, :] = right(odd).astype(BF16)
    AF[4 * ch + 1, rows, :] = even.astype(BF16)
    AF[4 * ch + 2, rows, :] = odd.astype(BF16)
    AF[4 * ch + 3, rows, :] = left(even).astype(BF16)


def spread(bb, k, n):
    return jnp.concatenate([bb[k]] * n, axis=0)


def store(ref, at, value, mask):
    if mask is not None:
        scale, start, stop = mask
        value = jnp.concatenate(
            [part for part in (value[:start], value[start:stop] * scale, value[stop:]) if part.shape[0]],
            axis=0,
        )
    ref[at : at + value.shape[0], :] = value.astype(BF16)


def first_layer(AF, at, w1, bias, HE, HO, to, mask=None):
    data = AF[:, at : at + 32, :].reshape(256, 256)
    for phase, H in enumerate((HE, HO)):
        got = jnp.dot(w1[512 * phase : 512 * phase + 512, :], data, preferred_element_type=F32)
        store(H, 32 * to, jnp.maximum(got + bias, 0.0), mask)


def down_layer(HE, HO, at, wd, bias, D, to, mask=None):
    even = jnp.dot(wd[0:96, 0:224], HE[32 * at : 32 * at + 224, :], preferred_element_type=F32)
    odd = jnp.dot(wd[96:288, 0:224], HO[32 * at : 32 * at + 224, :], preferred_element_type=F32)
    total = even + right(odd[0:96]) + odd[96:192] + bias
    store(D, 32 * to, jnp.maximum(total, 0.0), mask)


def deep_sum(F, at, w, bias):
    got = jnp.dot(w[...], F[32 * at : 32 * at + 256, :], preferred_element_type=F32)
    return got[192:384] + right(got[0:192]) + left(got[384:576]) + bias


def deep_layer(D, at, w, bias, T, to, mask=None):
    store(T, 32 * to, jnp.maximum(deep_sum(D, at, w, bias), 0.0), mask)


def last_layer(T, at, w, bias, FS, to):
    total = deep_sum(T, at, w, bias)
    for r in range(6):
        for part in range(4):
            for half in range(2):
                FS[half, part, 8 * (to + r) : 8 * (to + r) + 8, :] = total[
                    32 * r + 8 * part : 32 * r + 8 * part + 8, 128 * half : 128 * half + 128
                ]


def gather_rows(FS, start, count, O):
    for ch in range(32):
        for half in range(2):
            O[ch, :, 128 * half : 128 * half + 128] = FS[
                half, ch // 8, pl.ds(8 * start + ch % 8, count, stride=8), :
            ].astype(BF16)


def inner_kernel(enc, prior, w1, wd, wp, bb, O, keep_h, keep_d, keep_t, AF, HE, HO, D, T, FS):
    for k in range(8):
        fill(AF, 0, k, enc[16 * k : 16 * k + 16, :].astype(F32))
        fill(AF, 1, k, prior[k].astype(F32))
    bias = spread(bb, 0, 16)
    for g in range(7):
        first_layer(AF, 16 * g, w1, bias, HE, HO, 16 * g)
    for phase, H in enumerate((HE, HO)):
        keep_h[phase, 0] = H[0:128, :]
        keep_h[phase, 1] = H[3456:3584, :]
    bias = spread(bb, 1, 3)
    for g in range(18):
        down_layer(HE, HO, 6 * g + 2, wd, bias, D, 3 * g)
    keep_d[0] = D[0:256, :]
    keep_d[1] = D[1472:1728, :]
    bias = spread(bb, 2, 6)
    for g in range(8):
        deep_layer(D, 6 * g + 3, wp.at[0], bias, T, 6 * g)
    keep_t[0] = T[0:384, :]
    keep_t[1] = T[1152:1536, :]
    bias = spread(bb, 3, 6)
    for g in range(6):
        last_layer(T, 6 * g, wp.at[1], bias, FS, 6 * g)
    gather_rows(FS, 4, 32, O)


def make_inner(enc, prior, w1, wd, wp, bb):
    return pl.pallas_call(
        inner_kernel,
        out_shape=(
            jax.ShapeDtypeStruct((32, 32, 256), BF16),
            jax.ShapeDtypeStruct((2, 2, 128, 256), BF16),
            jax.ShapeDtypeStruct((2, 256, 256), BF16),
            jax.ShapeDtypeStruct((2, 384, 256), BF16),
        ),
        in_specs=[vspec()] * 6,
        out_specs=(vspec(),) * 4,
        scratch_shapes=[
            VMEM((8, 128, 256), BF16),
            VMEM((3584, 256), BF16),
            VMEM((3584, 256), BF16),
            VMEM((1728, 256), BF16),
            VMEM((1536, 256), BF16),
            VMEM((2, 4, 288, 128), F32),
        ],
        compiler_params=pltpu.CompilerParams(vmem_limit_bytes=16 << 20),
        cost_estimate=pl.CostEstimate(
            flops=6_000_000_000, bytes_accessed=4_000_000, transcendentals=0
        ),
        name="middle",
    )(enc, prior, w1, wd, wp, bb)


def outer_kernel(
    enc, prior, inner, outer, w1, wd, wp, bb, keep_h, keep_d, keep_t, got, out,
    AF, HE, HO, D, T, FS, O, sems,
):
    copies = [pltpu.make_async_copy(got, out.at[0, 0, :, pl.ds(16, 32), :], sems.at[2])]
    copies[0].start()
    place = lax.axis_index("rows")
    is_top = lax.rem(place, 2) == 0
    keep_first = jnp.where(place == 0, 0.0, 1.0)
    keep_last = jnp.where(place == 31, 0.0, 1.0)
    zeros8 = jnp.zeros((8, 512), F32)
    for ch in range(2):
        a = inner[ch].astype(F32)
        b = outer[ch].astype(F32)
        above = jnp.where(is_top, b[8:16], a[8:16])
        below = jnp.where(is_top, a[0:8], b[0:8])
        fill(AF.at[0], ch, 0, jnp.concatenate([zeros8, above], axis=0))
        fill(AF.at[1], ch, 1, jnp.concatenate([below, zeros8], axis=0))
    fill(AF.at[0], 0, 1, enc[0:16, :].astype(F32))
    fill(AF.at[0], 1, 1, prior[0].astype(F32))
    fill(AF.at[1], 0, 0, enc[112:128, :].astype(F32))
    fill(AF.at[1], 1, 0, prior[7].astype(F32))
    bias = spread(bb, 0, 16)
    for phase, H in enumerate((HE, HO)):
        H[0, 512:640, :] = keep_h[phase, 0]
        H[1, 0:128, :] = keep_h[phase, 1]
    first_layer(AF.at[0], 0, w1, bias, HE.at[0], HO.at[0], 0, (keep_first, 0, 160))
    first_layer(AF.at[1], 0, w1, bias, HE.at[1], HO.at[1], 4, (keep_last, 160, 512))
    bias = spread(bb, 1, 3)
    D[0, 288:544, :] = keep_d[0]
    D[1, 0:256, :] = keep_d[1]
    for g in range(3):
        mask = (keep_first, 0, 64) if g == 0 else None
        down_layer(HE.at[0], HO.at[0], 6 * g, wd, bias, D.at[0], 3 * g, mask)
    for g in range(2):
        mask = (keep_last, 0, 96) if g == 1 else None
        down_layer(HE.at[1], HO.at[1], 6 * g + 2, wd, bias, D.at[1], 3 * g + 8, mask)
    bias = spread(bb, 2, 6)
    T[0, 384:768, :] = keep_t[0]
    T[1, 0:384, :] = keep_t[1]
    for g in range(2):
        mask = (keep_first, 0, 32) if g == 0 else None
        deep_layer(D.at[0], 6 * g, wp.at[0], bias, T.at[0], 6 * g, mask)
    deep_layer(D.at[1], 5, wp.at[0], bias, T.at[1], 12, (keep_last, 160, 192))
    T[1, 576:768, :] = jnp.zeros((192, 256), BF16)
    bias = spread(bb, 3, 6)
    for side in range(2):
        for g in range(3):
            last_layer(T.at[side], 6 * g, wp.at[1], bias, FS.at[side], 6 * g)
        gather_rows(FS.at[side], 0, 16, O.at[side])
        copy = pltpu.make_async_copy(
            O.at[side], out.at[0, 0, :, pl.ds(48 * side, 16), :], sems.at[side]
        )
        copy.start()
        copies.append(copy)
    for copy in copies:
        copy.wait()


def make_outer(enc, prior, inner, outer, w1, wd, wp, bb, keep_h, keep_d, keep_t, got):
    hbm = pl.BlockSpec(memory_space=pltpu.HBM)
    return pl.pallas_call(
        outer_kernel,
        out_shape=jax.ShapeDtypeStruct((1, 1, 32, 64, 256), BF16),
        in_specs=[vspec()] * 12,
        out_specs=hbm,
        scratch_shapes=[
            VMEM((2, 8, 32, 256), BF16),
            VMEM((2, 640, 256), BF16),
            VMEM((2, 640, 256), BF16),
            VMEM((2, 544, 256), BF16),
            VMEM((2, 768, 256), BF16),
            VMEM((2, 2, 4, 144, 128), F32),
            VMEM((2, 32, 16, 256), BF16),
            pltpu.SemaphoreType.DMA((3,)),
        ],
        compiler_params=pltpu.CompilerParams(vmem_limit_bytes=16 << 20),
        name="border",
    )(enc, prior, inner, outer, w1, wd, wp, bb, keep_h, keep_d, keep_t, got)


def pairs(target):
    return [(i, target(i)) for i in range(32) if 0 <= target(i) < 32]


SWAP = pairs(lambda i: i ^ 1)
OUTWARD = pairs(lambda i: i - 2 if i % 2 == 0 else i + 2)
INWARD = pairs(lambda i: i + 2 if i % 2 == 0 else i - 2)
LAST = [(i, t) for i, t in INWARD if i % 2 == 1]
ACROSS = pairs(lambda i: i - 1 if i % 2 == 0 else i + 1)


def per_device(
    sections, block_offset, row_base, col_base, fractions, blend,
    conv_first, bias_first, conv_down, bias_down, conv_deep, bias_deep,
):
    def send(value, route):
        return lax.ppermute(value, "rows", route)

    own = sections[0, 0]
    p1 = send(own, OUTWARD)
    p2 = send(own, INWARD)
    a = send(own, SWAP)
    f1 = send(p1, OUTWARD)
    f2 = send(p2, LAST)
    sp1 = send(p1, SWAP)
    sp2 = send(p2, SWAP)
    sf1 = send(f1, SWAP)
    w1, wd, wp, bb = make_weights(
        conv_first, conv_down, conv_deep, bias_first, bias_down, bias_deep
    )
    pay, enc = make_warp(
        block_offset, row_base, col_base, fractions, blend,
        (own, a, p1, sp1, p2, sp2, f1, sf1, f2),
    )
    got = lax.all_to_all(pay, "gz", 0, 0)
    given = make_prior(got)
    prior = lax.all_to_all(given, "gz", 0, 0)
    edges = jnp.stack(
        [
            jnp.concatenate([enc[0:8], enc[120:128]], axis=0),
            jnp.concatenate([prior[0, 0:8], prior[7, 8:16]], axis=0),
        ]
    )
    inner = send(edges, SWAP)
    outer = send(edges, ACROSS)
    got, keep_h, keep_d, keep_t = make_inner(enc, prior, w1, wd, wp, bb)
    return make_outer(
        enc, prior, inner, outer, w1, wd, wp, bb, keep_h, keep_d, keep_t, got
    )


def solution(mesh):
    return jax.shard_map(
        per_device,
        mesh=mesh,
        in_specs=(
            P(None, "gz", "rows", None),
            P(None, "gz", "rows", None),
            P(None, "gz", "rows", None),
            P(None, "gz", "rows", None),
            P(None, None, "gz", "rows", None),
            P(None, "gz"),
            P(), P(), P(), P(), P(), P(),
        ),
        out_specs=P(None, "gz", None, "rows", None),
        check_vma=False,
    )
```

```python
import jax
import jax.numpy as jnp
from jax import lax
from jax.experimental import pallas as pl
from jax.experimental.pallas import tpu as pltpu
from jax.sharding import PartitionSpec as P

F32 = jnp.float32
BF16 = jnp.bfloat16
VMEM = pltpu.VMEM


def vspec():
    return pl.BlockSpec(memory_space=pltpu.VMEM)


def sspec():
    return pl.BlockSpec(memory_space=pltpu.SMEM)


def iota(shape, dim):
    return lax.broadcasted_iota(jnp.int32, shape, dim)


def weights_kernel(kf, kd, kp, bf, bd, bp, w1, wd, wp, bb):
    row = iota((32, 256), 0)
    lane = iota((32, 256), 1)

    def place(dr):
        return jnp.where(lane == row + 32 * dr, 1.0, 0.0).astype(BF16)

    spots = [place(dr) for dr in range(3)]

    def base(taps):
        return sum(jnp.dot(taps[dr], spots[dr], preferred_element_type=F32) for dr in range(3))

    diagonal = iota((32, 32), 0) == iota((32, 32), 1)

    def upright(line):
        return jnp.sum(jnp.where(diagonal, line, 0.0), axis=1, keepdims=True)

    within = lane & 31
    quarter = (lane >> 5) & 3
    for phase in range(2):
        acc = jnp.zeros((32, 256), F32)
        for dr in range(3):
            for dx in range(3):
                tap = kf[3 * dr + dx].astype(F32)
                value = jnp.where(lane < 128, upright(tap[0:1, :]), upright(tap[1:2, :]))
                hit = (quarter == dx + phase) & (within == 10 + dr)
                acc = acc + jnp.where(hit, value, 0.0)
        for r in range(16):
            moved = acc if r == 0 else pltpu.roll(acc, r, 1)
            w1[pl.ds(phase * 512 + r * 32, 32), :] = moved.astype(BF16)
    for place_at, dx in enumerate((1, 0, 2)):
        acc = base([kd[3 * dr + dx] for dr in range(3)])
        for r in range(3):
            moved = acc if r == 0 else pltpu.roll(acc, 64 * r, 1)
            wd[pl.ds(place_at * 96 + r * 32, 32), :] = moved.astype(BF16)
    for layer in range(2):
        for dx in range(3):
            acc = base([kp[layer, 3 * dr + dx] for dr in range(3)])
            for r in range(6):
                moved = acc if r == 0 else pltpu.roll(acc, 32 * r, 1)
                wp[layer, pl.ds(dx * 192 + r * 32, 32), :] = moved.astype(BF16)
    for k, line in enumerate((bf[...], bd[...], bp[0:1, :], bp[1:2, :])):
        bb[k] = jnp.broadcast_to(upright(line), (32, 256))


def make_weights(conv_first, conv_down, conv_deep, bias_first, bias_down, bias_deep):
    return pl.pallas_call(
        weights_kernel,
        out_shape=(
            jax.ShapeDtypeStruct((1024, 256), BF16),
            jax.ShapeDtypeStruct((288, 256), BF16),
            jax.ShapeDtypeStruct((2, 576, 256), BF16),
            jax.ShapeDtypeStruct((4, 32, 256), F32),
        ),
        in_specs=[vspec()] * 6,
        out_specs=(vspec(),) * 4,
        cost_estimate=pl.CostEstimate(flops=20_000_000, bytes_accessed=2_000_000, transcendentals=0),
        compiler_params=pltpu.CompilerParams(vmem_limit_bytes=6 << 20),
        name="weights",
    )(conv_first.transpose(0, 2, 1), conv_down, conv_deep, bias_first[None], bias_down[None], bias_deep)


OFFSETS = (0, 1, 2, -1, -2, 3, 4, -3, -4)


def hold_kernel(own, held, sem):
    fetch = pltpu.make_async_copy(own, held, sem)
    fetch.start()
    fetch.wait()


def make_hold(own):
    own = pltpu.with_memory_space_constraint(own, pltpu.HBM)
    return pl.pallas_call(
        hold_kernel,
        out_shape=jax.ShapeDtypeStruct((128, 512), BF16),
        in_specs=[pl.BlockSpec(memory_space=pltpu.HBM)],
        out_specs=vspec(),
        scratch_shapes=[pltpu.SemaphoreType.DMA],
        compiler_params=pltpu.CompilerParams(vmem_limit_bytes=4 << 20),
        name="hold",
    )(own)


def warp_kernel(offs, base, cols, frac, blend, *refs):
    blocks, (pay, enc, S, MJ, MV) = refs[:9], refs[9:]
    core = lax.rem(lax.axis_index("rows"), 2)
    sign = 1 - 2 * core
    for k, off in enumerate(OFFSETS):
        S[4 + sign * off] = blocks[k][...]
    mats = []
    for j in range(4):
        lo, hi = max(j - 1, 0), min(j + 1, 3)
        wide = (hi - lo + 1) * 128
        src = iota((wide, 128), 0) + (lo - j) * 128
        n = iota((wide, 128), 1)
        if j % 2 == 0:
            x = jnp.where(n < 64, 2 * n, 2 * n - 127)
        else:
            x = jnp.where(n < 64, 2 * n + 1, 2 * n - 128)
        q = frac[1, 0, 0, 0, j].astype(F32) * (1.0 / 256.0)
        target = cols[0, 0, 0, j] + x
        mat = jnp.where(src == target, 1.0 - q, 0.0) + jnp.where(src == target + 1, q, 0.0)
        mats.append(mat.astype(BF16))
    for j in range(4):
        lo, hi = max(j - 1, 0), min(j + 1, 3)
        first = offs[0, 0, 0, j] + 4
        window = S[pl.ds(first, 2), :, lo * 128 : (hi + 1) * 128].reshape(256, (hi - lo + 1) * 128)
        out = jnp.dot(window, mats[j], preferred_element_type=F32)
        MJ[j, 0:256, :] = out.astype(BF16).astype(F32)
    lane1 = iota((136, 128), 1)
    for pair in range(2):
        a = MJ[2 * pair, pl.ds(base[0, 0, 0, 2 * pair], 136), :]
        b = MJ[2 * pair + 1, pl.ds(base[0, 0, 0, 2 * pair + 1], 136), :]
        MV[:, pair * 128 : (pair + 1) * 128] = jnp.where(lane1 < 64, a, b)
        MV[:, 256 + pair * 128 : 256 + (pair + 1) * 128] = pltpu.roll(
            jnp.where(lane1 < 64, b, a), 64, 1
        )
    lane = iota((8, 512), 1)
    which = (lane >> 6) & 3
    p = jnp.zeros((8, 512), F32)
    for j in range(4):
        p = jnp.where(which == j, frac[0, 0, 0, 0, j].astype(F32) * (1.0 / 256.0), p)
    rate = jnp.full((16, 128), blend[0, 0], F32)
    top = rate.astype(BF16).astype(F32)
    mid = (rate - top).astype(BF16).astype(F32)
    low = rate - top - mid
    row = iota((16, 128), 0)
    extra = jnp.where(row == 8, top, jnp.where(row == 9, mid, jnp.where(row == 10, low, 0.0)))
    for c in range(4):
        extra = jnp.where(row == 4 + c, p[0:1, 128 * c : 128 * c + 128], extra)
    p16 = jnp.concatenate([p, p], axis=0)
    for k in range(8):
        here = MV[16 * k : 16 * k + 16, :]
        below = MV[16 * k + 1 : 16 * k + 17, :]
        enc[16 * k : 16 * k + 16, :] = ((1.0 - p16) * here + p16 * below).astype(BF16)
        pay[k, :, 0:512] = here.astype(BF16)
        tail = extra
        for c in range(4):
            piece = MV[16 * k + 16 : 16 * k + 17, 128 * c : 128 * c + 128]
            tail = jnp.where(row == c, piece, tail)
        pay[k, :, 512:640] = tail.astype(BF16)


def make_warp(offs, base, cols, frac, blend, blocks):
    return pl.pallas_call(
        warp_kernel,
        out_shape=(
            jax.ShapeDtypeStruct((8, 16, 640), BF16),
            jax.ShapeDtypeStruct((128, 512), BF16),
        ),
        in_specs=[sspec()] * 5 + [vspec()] * 9,
        out_specs=(vspec(), vspec()),
        scratch_shapes=[
            VMEM((9, 128, 512), BF16),
            VMEM((4, 264, 128), F32),
            VMEM((136, 512), F32),
        ],
        compiler_params=pltpu.CompilerParams(vmem_limit_bytes=8 << 20),
        name="warp",
    )(offs, base, cols, frac, blend, *blocks)


def prior_kernel(got, out, M):
    state = jnp.zeros((16, 512), F32)
    for s in range(8):
        out[s] = state.astype(BF16)
        if s == 7:
            break
        M[s, 0:16, :] = got[s, :, 0:512].astype(F32)
        extra = got[s, :, 512:640].astype(F32)
        for c in range(4):
            M[s, 16:17, 128 * c : 128 * c + 128] = extra[c : c + 1, :]
        p = jnp.concatenate([extra[4 + c : 5 + c, :] for c in range(4)], axis=1)
        rate = extra[8:9, 0:1] + extra[9:10, 0:1] + extra[10:11, 0:1]
        warped = (1.0 - p) * M[s, 0:16, :] + p * M[s, 1:17, :]
        state = rate * state + (1.0 - rate) * warped


def make_prior(got):
    return pl.pallas_call(
        prior_kernel,
        out_shape=jax.ShapeDtypeStruct((8, 16, 512), BF16),
        in_specs=[vspec()],
        out_specs=vspec(),
        scratch_shapes=[VMEM((7, 24, 512), F32)],
        compiler_params=pltpu.CompilerParams(vmem_limit_bytes=4 << 20),
        name="prior",
    )(got)


def right(v):
    at = iota(v.shape, 1)
    return jnp.where(at == 0, 0.0, pltpu.roll(v, 1, 1))


def left(v):
    at = iota(v.shape, 1)
    return jnp.where(at == 255, 0.0, pltpu.roll(v, 255, 1))


def fill(AF, ch, tile, value):
    even, odd = value[:, :256], value[:, 256:]
    rows = pl.ds(16 * tile, 16)
    AF[4 * ch, rows, :] = right(odd).astype(BF16)
    AF[4 * ch + 1, rows, :] = even.astype(BF16)
    AF[4 * ch + 2, rows, :] = odd.astype(BF16)
    AF[4 * ch + 3, rows, :] = left(even).astype(BF16)


def spread(bb, k, n):
    return jnp.concatenate([bb[k]] * n, axis=0)


def store(ref, at, value, mask):
    if mask is not None:
        scale, start, stop = mask
        value = jnp.concatenate(
            [part for part in (value[:start], value[start:stop] * scale, value[stop:]) if part.shape[0]],
            axis=0,
        )
    ref[at : at + value.shape[0], :] = value.astype(BF16)


def first_layer(AF, at, w1, bias, HE, HO, to, mask=None):
    data = AF[:, at : at + 32, :].reshape(256, 256)
    for phase, H in enumerate((HE, HO)):
        got = jnp.dot(w1[512 * phase : 512 * phase + 512, :], data, preferred_element_type=F32)
        store(H, 32 * to, jnp.maximum(got + bias, 0.0), mask)


def down_layer(HE, HO, at, wd, bias, D, to, mask=None):
    even = jnp.dot(wd[0:96, 0:224], HE[32 * at : 32 * at + 224, :], preferred_element_type=F32)
    odd = jnp.dot(wd[96:288, 0:224], HO[32 * at : 32 * at + 224, :], preferred_element_type=F32)
    total = even + right(odd[0:96]) + odd[96:192] + bias
    store(D, 32 * to, jnp.maximum(total, 0.0), mask)


def deep_sum(F, at, w, bias):
    got = jnp.dot(w[...], F[32 * at : 32 * at + 256, :], preferred_element_type=F32)
    return got[192:384] + right(got[0:192]) + left(got[384:576]) + bias


def deep_layer(D, at, w, bias, T, to, mask=None):
    store(T, 32 * to, jnp.maximum(deep_sum(D, at, w, bias), 0.0), mask)


def last_layer(T, at, w, bias, FS, to):
    total = deep_sum(T, at, w, bias)
    for r in range(6):
        for part in range(4):
            for half in range(2):
                FS[half, part, 8 * (to + r) : 8 * (to + r) + 8, :] = total[
                    32 * r + 8 * part : 32 * r + 8 * part + 8, 128 * half : 128 * half + 128
                ]


def gather_rows(FS, start, count, O):
    for ch in range(32):
        for half in range(2):
            O[ch, :, 128 * half : 128 * half + 128] = FS[
                half, ch // 8, pl.ds(8 * start + ch % 8, count, stride=8), :
            ].astype(BF16)


def inner_kernel(enc, prior, w1, wd, wp, bb, O, keep_h, keep_d, keep_t, AF, HE, HO, D, T, FS):
    for k in range(8):
        fill(AF, 0, k, enc[16 * k : 16 * k + 16, :].astype(F32))
        fill(AF, 1, k, prior[k].astype(F32))
    bias = spread(bb, 0, 16)
    for g in range(7):
        first_layer(AF, 16 * g, w1, bias, HE, HO, 16 * g)
    for phase, H in enumerate((HE, HO)):
        keep_h[phase, 0] = H[0:128, :]
        keep_h[phase, 1] = H[3456:3584, :]
    bias = spread(bb, 1, 3)
    for g in range(18):
        down_layer(HE, HO, 6 * g + 2, wd, bias, D, 3 * g)
    keep_d[0] = D[0:256, :]
    keep_d[1] = D[1472:1728, :]
    bias = spread(bb, 2, 6)
    for g in range(8):
        deep_layer(D, 6 * g + 3, wp.at[0], bias, T, 6 * g)
    keep_t[0] = T[0:384, :]
    keep_t[1] = T[1152:1536, :]
    bias = spread(bb, 3, 6)
    for g in range(6):
        last_layer(T, 6 * g, wp.at[1], bias, FS, 6 * g)
    gather_rows(FS, 4, 32, O)


def make_inner(enc, prior, w1, wd, wp, bb):
    return pl.pallas_call(
        inner_kernel,
        out_shape=(
            jax.ShapeDtypeStruct((32, 32, 256), BF16),
            jax.ShapeDtypeStruct((2, 2, 128, 256), BF16),
            jax.ShapeDtypeStruct((2, 256, 256), BF16),
            jax.ShapeDtypeStruct((2, 384, 256), BF16),
        ),
        in_specs=[vspec()] * 6,
        out_specs=(vspec(),) * 4,
        scratch_shapes=[
            VMEM((8, 128, 256), BF16),
            VMEM((3584, 256), BF16),
            VMEM((3584, 256), BF16),
            VMEM((1728, 256), BF16),
            VMEM((1536, 256), BF16),
            VMEM((2, 4, 288, 128), F32),
        ],
        compiler_params=pltpu.CompilerParams(vmem_limit_bytes=16 << 20),
        cost_estimate=pl.CostEstimate(
            flops=6_000_000_000, bytes_accessed=4_000_000, transcendentals=0
        ),
        name="middle",
    )(enc, prior, w1, wd, wp, bb)


def outer_kernel(
    enc, prior, inner, outer, w1, wd, wp, bb, keep_h, keep_d, keep_t, got, out,
    AF, HE, HO, D, T, FS, O, sems,
):
    copies = [pltpu.make_async_copy(got, out.at[0, 0, :, pl.ds(16, 32), :], sems.at[2])]
    copies[0].start()
    place = lax.axis_index("rows")
    is_top = lax.rem(place, 2) == 0
    keep_first = jnp.where(place == 0, 0.0, 1.0)
    keep_last = jnp.where(place == 31, 0.0, 1.0)
    zeros8 = jnp.zeros((8, 512), F32)
    for ch in range(2):
        a = inner[ch].astype(F32)
        b = outer[ch].astype(F32)
        above = jnp.where(is_top, b[8:16], a[8:16])
        below = jnp.where(is_top, a[0:8], b[0:8])
        fill(AF.at[0], ch, 0, jnp.concatenate([zeros8, above], axis=0))
        fill(AF.at[1], ch, 1, jnp.concatenate([below, zeros8], axis=0))
    fill(AF.at[0], 0, 1, enc[0:16, :].astype(F32))
    fill(AF.at[0], 1, 1, prior[0].astype(F32))
    fill(AF.at[1], 0, 0, enc[112:128, :].astype(F32))
    fill(AF.at[1], 1, 0, prior[7].astype(F32))
    bias = spread(bb, 0, 16)
    for phase, H in enumerate((HE, HO)):
        H[0, 512:640, :] = keep_h[phase, 0]
        H[1, 0:128, :] = keep_h[phase, 1]
    first_layer(AF.at[0], 0, w1, bias, HE.at[0], HO.at[0], 0, (keep_first, 0, 160))
    first_layer(AF.at[1], 0, w1, bias, HE.at[1], HO.at[1], 4, (keep_last, 160, 512))
    bias = spread(bb, 1, 3)
    D[0, 288:544, :] = keep_d[0]
    D[1, 0:256, :] = keep_d[1]
    for g in range(3):
        mask = (keep_first, 0, 64) if g == 0 else None
        down_layer(HE.at[0], HO.at[0], 6 * g, wd, bias, D.at[0], 3 * g, mask)
    for g in range(2):
        mask = (keep_last, 0, 96) if g == 1 else None
        down_layer(HE.at[1], HO.at[1], 6 * g + 2, wd, bias, D.at[1], 3 * g + 8, mask)
    bias = spread(bb, 2, 6)
    T[0, 384:768, :] = keep_t[0]
    T[1, 0:384, :] = keep_t[1]
    for g in range(2):
        mask = (keep_first, 0, 32) if g == 0 else None
        deep_layer(D.at[0], 6 * g, wp.at[0], bias, T.at[0], 6 * g, mask)
    deep_layer(D.at[1], 5, wp.at[0], bias, T.at[1], 12, (keep_last, 160, 192))
    T[1, 576:768, :] = jnp.zeros((192, 256), BF16)
    bias = spread(bb, 3, 6)
    for side in range(2):
        for g in range(3):
            last_layer(T.at[side], 6 * g, wp.at[1], bias, FS.at[side], 6 * g)
        gather_rows(FS.at[side], 0, 16, O.at[side])
        copy = pltpu.make_async_copy(
            O.at[side], out.at[0, 0, :, pl.ds(48 * side, 16), :], sems.at[side]
        )
        copy.start()
        copies.append(copy)
    for copy in copies:
        copy.wait()


def make_outer(enc, prior, inner, outer, w1, wd, wp, bb, keep_h, keep_d, keep_t, got):
    hbm = pl.BlockSpec(memory_space=pltpu.HBM)
    return pl.pallas_call(
        outer_kernel,
        out_shape=jax.ShapeDtypeStruct((1, 1, 32, 64, 256), BF16),
        in_specs=[vspec()] * 12,
        out_specs=hbm,
        scratch_shapes=[
            VMEM((2, 8, 32, 256), BF16),
            VMEM((2, 640, 256), BF16),
            VMEM((2, 640, 256), BF16),
            VMEM((2, 544, 256), BF16),
            VMEM((2, 768, 256), BF16),
            VMEM((2, 2, 4, 144, 128), F32),
            VMEM((2, 32, 16, 256), BF16),
            pltpu.SemaphoreType.DMA((3,)),
        ],
        compiler_params=pltpu.CompilerParams(vmem_limit_bytes=16 << 20),
        name="border",
    )(enc, prior, inner, outer, w1, wd, wp, bb, keep_h, keep_d, keep_t, got)


def pairs(target):
    return [(i, target(i)) for i in range(32) if 0 <= target(i) < 32]


SWAP = pairs(lambda i: i ^ 1)
OUTWARD = pairs(lambda i: i - 2 if i % 2 == 0 else i + 2)
INWARD = pairs(lambda i: i + 2 if i % 2 == 0 else i - 2)
LAST = [(i, t) for i, t in INWARD if i % 2 == 1]
ACROSS = pairs(lambda i: i - 1 if i % 2 == 0 else i + 1)


def per_device(
    sections, block_offset, row_base, col_base, fractions, blend,
    conv_first, bias_first, conv_down, bias_down, conv_deep, bias_deep,
):
    def send(value, route):
        return lax.ppermute(value, "rows", route)

    own = sections[0, 0]
    p1 = send(own, OUTWARD)
    p2 = send(own, INWARD)
    a = send(own, SWAP)
    f1 = send(p1, OUTWARD)
    f2 = send(p2, LAST)
    sp1 = send(p1, SWAP)
    sp2 = send(p2, SWAP)
    sf1 = send(f1, SWAP)
    w1, wd, wp, bb = make_weights(
        conv_first, conv_down, conv_deep, bias_first, bias_down, bias_deep
    )
    held = make_hold(own)
    pay, enc = make_warp(
        block_offset, row_base, col_base, fractions, blend,
        (held, a, p1, sp1, p2, sp2, f1, sf1, f2),
    )
    got = lax.all_to_all(pay, "gz", 0, 0)
    given = make_prior(got)
    prior = lax.all_to_all(given, "gz", 0, 0)
    edges = jnp.stack(
        [
            jnp.concatenate([enc[0:8], enc[120:128]], axis=0),
            jnp.concatenate([prior[0, 0:8], prior[7, 8:16]], axis=0),
        ]
    )
    inner = send(edges, SWAP)
    outer = send(edges, ACROSS)
    got, keep_h, keep_d, keep_t = make_inner(enc, prior, w1, wd, wp, bb)
    return make_outer(
        enc, prior, inner, outer, w1, wd, wp, bb, keep_h, keep_d, keep_t, got
    )


def solution(mesh):
    return jax.shard_map(
        per_device,
        mesh=mesh,
        in_specs=(
            P(None, "gz", "rows", None),
            P(None, "gz", "rows", None),
            P(None, "gz", "rows", None),
            P(None, "gz", "rows", None),
            P(None, None, "gz", "rows", None),
            P(None, "gz"),
            P(), P(), P(), P(), P(), P(),
        ),
        out_specs=P(None, "gz", None, "rows", None),
        check_vma=False,
    )
```

```python
import jax
import jax.numpy as jnp
from jax import lax
from jax.experimental import pallas as pl
from jax.experimental.pallas import tpu as pltpu
from jax.sharding import PartitionSpec as P

F32 = jnp.float32
BF16 = jnp.bfloat16
VMEM = pltpu.VMEM


def vspec():
    return pl.BlockSpec(memory_space=pltpu.VMEM)


def sspec():
    return pl.BlockSpec(memory_space=pltpu.SMEM)


def iota(shape, dim):
    return lax.broadcasted_iota(jnp.int32, shape, dim)


def weights_kernel(kf, kd, kp, bf, bd, bp, w1, wd, wp, bb):
    row = iota((32, 256), 0)
    lane = iota((32, 256), 1)

    def place(dr):
        return jnp.where(lane == row + 32 * dr, 1.0, 0.0).astype(BF16)

    spots = [place(dr) for dr in range(3)]

    def base(taps):
        return sum(jnp.dot(taps[dr], spots[dr], preferred_element_type=F32) for dr in range(3))

    diagonal = iota((32, 32), 0) == iota((32, 32), 1)

    def upright(line):
        return jnp.sum(jnp.where(diagonal, line, 0.0), axis=1, keepdims=True)

    within = lane & 31
    quarter = (lane >> 5) & 3
    for phase in range(2):
        acc = jnp.zeros((32, 256), F32)
        for dr in range(3):
            for dx in range(3):
                tap = kf[3 * dr + dx].astype(F32)
                value = jnp.where(lane < 128, upright(tap[0:1, :]), upright(tap[1:2, :]))
                hit = (quarter == dx + phase) & (within == 10 + dr)
                acc = acc + jnp.where(hit, value, 0.0)
        for r in range(16):
            moved = acc if r == 0 else pltpu.roll(acc, r, 1)
            w1[pl.ds(phase * 512 + r * 32, 32), :] = moved.astype(BF16)
    for place_at, dx in enumerate((1, 0, 2)):
        acc = base([kd[3 * dr + dx] for dr in range(3)])
        for r in range(3):
            moved = acc if r == 0 else pltpu.roll(acc, 64 * r, 1)
            wd[pl.ds(place_at * 96 + r * 32, 32), :] = moved.astype(BF16)
    for layer in range(2):
        for dx in range(3):
            acc = base([kp[layer, 3 * dr + dx] for dr in range(3)])
            for r in range(6):
                moved = acc if r == 0 else pltpu.roll(acc, 32 * r, 1)
                wp[layer, pl.ds(dx * 192 + r * 32, 32), :] = moved.astype(BF16)
    for k, line in enumerate((bf[...], bd[...], bp[0:1, :], bp[1:2, :])):
        bb[k] = jnp.broadcast_to(upright(line), (32, 256))


def make_weights(conv_first, conv_down, conv_deep, bias_first, bias_down, bias_deep):
    return pl.pallas_call(
        weights_kernel,
        out_shape=(
            jax.ShapeDtypeStruct((1024, 256), BF16),
            jax.ShapeDtypeStruct((288, 256), BF16),
            jax.ShapeDtypeStruct((2, 576, 256), BF16),
            jax.ShapeDtypeStruct((4, 32, 256), F32),
        ),
        in_specs=[vspec()] * 6,
        out_specs=(vspec(),) * 4,
        cost_estimate=pl.CostEstimate(flops=20_000_000, bytes_accessed=2_000_000, transcendentals=0),
        compiler_params=pltpu.CompilerParams(vmem_limit_bytes=6 << 20),
        name="weights",
    )(conv_first.transpose(0, 2, 1), conv_down, conv_deep, bias_first[None], bias_down[None], bias_deep)


OFFSETS = (0, 1, 2, -1, -2, 3, 4, -3, -4)


def hold_kernel(own, held, sem):
    fetch = pltpu.make_async_copy(own, held, sem)
    fetch.start()
    fetch.wait()


def make_hold(own):
    own = pltpu.with_memory_space_constraint(own, pltpu.HBM)
    return pl.pallas_call(
        hold_kernel,
        out_shape=jax.ShapeDtypeStruct((128, 512), BF16),
        in_specs=[pl.BlockSpec(memory_space=pltpu.HBM)],
        out_specs=vspec(),
        scratch_shapes=[pltpu.SemaphoreType.DMA],
        compiler_params=pltpu.CompilerParams(vmem_limit_bytes=4 << 20),
        name="hold",
    )(own)


def warp_kernel(offs, base, cols, frac, blend, *refs):
    blocks, (pay, enc, S, MJ, MV) = refs[:9], refs[9:]
    core = lax.rem(lax.axis_index("rows"), 2)
    sign = 1 - 2 * core
    for k, off in enumerate(OFFSETS):
        S[4 + sign * off] = blocks[k][...]
    mats = []
    for j in range(4):
        lo, hi = max(j - 1, 0), min(j + 1, 3)
        wide = (hi - lo + 1) * 128
        src = iota((wide, 128), 0) + (lo - j) * 128
        n = iota((wide, 128), 1)
        if j % 2 == 0:
            x = jnp.where(n < 64, 2 * n, 2 * n - 127)
        else:
            x = jnp.where(n < 64, 2 * n + 1, 2 * n - 128)
        q = frac[1, 0, 0, 0, j].astype(F32) * (1.0 / 256.0)
        target = cols[0, 0, 0, j] + x
        mat = jnp.where(src == target, 1.0 - q, 0.0) + jnp.where(src == target + 1, q, 0.0)
        mats.append(mat.astype(BF16))
    for j in range(4):
        lo, hi = max(j - 1, 0), min(j + 1, 3)
        first = offs[0, 0, 0, j] + 4
        window = S[pl.ds(first, 2), :, lo * 128 : (hi + 1) * 128].reshape(256, (hi - lo + 1) * 128)
        out = jnp.dot(window, mats[j], preferred_element_type=F32)
        MJ[j, 0:256, :] = out.astype(BF16).astype(F32)
    lane1 = iota((136, 128), 1)
    for pair in range(2):
        a = MJ[2 * pair, pl.ds(base[0, 0, 0, 2 * pair], 136), :]
        b = MJ[2 * pair + 1, pl.ds(base[0, 0, 0, 2 * pair + 1], 136), :]
        MV[:, pair * 128 : (pair + 1) * 128] = jnp.where(lane1 < 64, a, b)
        MV[:, 256 + pair * 128 : 256 + (pair + 1) * 128] = pltpu.roll(
            jnp.where(lane1 < 64, b, a), 64, 1
        )
    lane = iota((8, 512), 1)
    which = (lane >> 6) & 3
    p = jnp.zeros((8, 512), F32)
    for j in range(4):
        p = jnp.where(which == j, frac[0, 0, 0, 0, j].astype(F32) * (1.0 / 256.0), p)
    rate = jnp.full((16, 128), blend[0, 0], F32)
    top = rate.astype(BF16).astype(F32)
    mid = (rate - top).astype(BF16).astype(F32)
    low = rate - top - mid
    row = iota((16, 128), 0)
    extra = jnp.where(row == 8, top, jnp.where(row == 9, mid, jnp.where(row == 10, low, 0.0)))
    for c in range(4):
        extra = jnp.where(row == 4 + c, p[0:1, 128 * c : 128 * c + 128], extra)
    p16 = jnp.concatenate([p, p], axis=0)
    for k in range(8):
        here = MV[16 * k : 16 * k + 16, :]
        below = MV[16 * k + 1 : 16 * k + 17, :]
        enc[16 * k : 16 * k + 16, :] = ((1.0 - p16) * here + p16 * below).astype(BF16)
        pay[k, :, 0:512] = here.astype(BF16)
        tail = extra
        for c in range(4):
            piece = MV[16 * k + 16 : 16 * k + 17, 128 * c : 128 * c + 128]
            tail = jnp.where(row == c, piece, tail)
        pay[k, :, 512:640] = tail.astype(BF16)


def make_warp(offs, base, cols, frac, blend, blocks):
    return pl.pallas_call(
        warp_kernel,
        out_shape=(
            jax.ShapeDtypeStruct((8, 16, 640), BF16),
            jax.ShapeDtypeStruct((128, 512), BF16),
        ),
        in_specs=[sspec()] * 5 + [vspec()] * 9,
        out_specs=(vspec(), vspec()),
        scratch_shapes=[
            VMEM((9, 128, 512), BF16),
            VMEM((4, 264, 128), F32),
            VMEM((136, 512), F32),
        ],
        compiler_params=pltpu.CompilerParams(vmem_limit_bytes=8 << 20),
        name="warp",
    )(offs, base, cols, frac, blend, *blocks)


def prior_kernel(got, given, M, out, sems):
    copies = [pltpu.make_async_copy(out.at[s], given.at[s], sems.at[s]) for s in range(8)]
    state = jnp.zeros((16, 512), F32)
    for s in range(8):
        out[s] = state.astype(BF16)
        copies[s].start()
        if s == 7:
            break
        M[s, 0:16, :] = got[s, :, 0:512].astype(F32)
        extra = got[s, :, 512:640].astype(F32)
        for c in range(4):
            M[s, 16:17, 128 * c : 128 * c + 128] = extra[c : c + 1, :]
        p = jnp.concatenate([extra[4 + c : 5 + c, :] for c in range(4)], axis=1)
        rate = extra[8:9, 0:1] + extra[9:10, 0:1] + extra[10:11, 0:1]
        warped = (1.0 - p) * M[s, 0:16, :] + p * M[s, 1:17, :]
        state = rate * state + (1.0 - rate) * warped
    for copy in copies:
        copy.wait()


def make_prior(got):
    return pl.pallas_call(
        prior_kernel,
        out_shape=jax.ShapeDtypeStruct((8, 16, 512), BF16),
        in_specs=[vspec()],
        out_specs=pl.BlockSpec(memory_space=pltpu.HBM),
        scratch_shapes=[VMEM((7, 24, 512), F32), VMEM((8, 16, 512), BF16), pltpu.SemaphoreType.DMA((8,))],
        compiler_params=pltpu.CompilerParams(vmem_limit_bytes=4 << 20),
        name="prior",
    )(got)


def right(v):
    at = iota(v.shape, 1)
    return jnp.where(at == 0, 0.0, pltpu.roll(v, 1, 1))


def left(v):
    at = iota(v.shape, 1)
    return jnp.where(at == 255, 0.0, pltpu.roll(v, 255, 1))


def fill(AF, ch, tile, value):
    even, odd = value[:, :256], value[:, 256:]
    rows = pl.ds(16 * tile, 16)
    AF[4 * ch, rows, :] = right(odd).astype(BF16)
    AF[4 * ch + 1, rows, :] = even.astype(BF16)
    AF[4 * ch + 2, rows, :] = odd.astype(BF16)
    AF[4 * ch + 3, rows, :] = left(even).astype(BF16)


def spread(bb, k, n):
    return jnp.concatenate([bb[k]] * n, axis=0)


def store(ref, at, value, mask):
    if mask is not None:
        scale, start, stop = mask
        value = jnp.concatenate(
            [part for part in (value[:start], value[start:stop] * scale, value[stop:]) if part.shape[0]],
            axis=0,
        )
    ref[at : at + value.shape[0], :] = value.astype(BF16)


def first_layer(AF, at, w1, bias, HE, HO, to, mask=None):
    data = AF[:, at : at + 32, :].reshape(256, 256)
    for phase, H in enumerate((HE, HO)):
        got = jnp.dot(w1[512 * phase : 512 * phase + 512, :], data, preferred_element_type=F32)
        store(H, 32 * to, jnp.maximum(got + bias, 0.0), mask)


def down_layer(HE, HO, at, wd, bias, D, to, mask=None):
    even = jnp.dot(wd[0:96, 0:224], HE[32 * at : 32 * at + 224, :], preferred_element_type=F32)
    odd = jnp.dot(wd[96:288, 0:224], HO[32 * at : 32 * at + 224, :], preferred_element_type=F32)
    total = even + right(odd[0:96]) + odd[96:192] + bias
    store(D, 32 * to, jnp.maximum(total, 0.0), mask)


def deep_sum(F, at, w, bias):
    got = jnp.dot(w[...], F[32 * at : 32 * at + 256, :], preferred_element_type=F32)
    return got[192:384] + right(got[0:192]) + left(got[384:576]) + bias


def deep_layer(D, at, w, bias, T, to, mask=None):
    store(T, 32 * to, jnp.maximum(deep_sum(D, at, w, bias), 0.0), mask)


def last_layer(T, at, w, bias, FS, to):
    total = deep_sum(T, at, w, bias)
    for r in range(6):
        for part in range(4):
            for half in range(2):
                FS[half, part, 8 * (to + r) : 8 * (to + r) + 8, :] = total[
                    32 * r + 8 * part : 32 * r + 8 * part + 8, 128 * half : 128 * half + 128
                ]


def gather_rows(FS, start, count, O):
    for ch in range(32):
        for half in range(2):
            O[ch, :, 128 * half : 128 * half + 128] = FS[
                half, ch // 8, pl.ds(8 * start + ch % 8, count, stride=8), :
            ].astype(BF16)


def inner_kernel(enc, prior, w1, wd, wp, bb, O, keep_h, keep_d, keep_t, AF, HE, HO, D, T, FS):
    for k in range(8):
        fill(AF, 0, k, enc[16 * k : 16 * k + 16, :].astype(F32))
        fill(AF, 1, k, prior[k].astype(F32))
    bias = spread(bb, 0, 16)
    for g in range(7):
        first_layer(AF, 16 * g, w1, bias, HE, HO, 16 * g)
    for phase, H in enumerate((HE, HO)):
        keep_h[phase, 0] = H[0:128, :]
        keep_h[phase, 1] = H[3456:3584, :]
    bias = spread(bb, 1, 3)
    for g in range(18):
        down_layer(HE, HO, 6 * g + 2, wd, bias, D, 3 * g)
    keep_d[0] = D[0:256, :]
    keep_d[1] = D[1472:1728, :]
    bias = spread(bb, 2, 6)
    for g in range(8):
        deep_layer(D, 6 * g + 3, wp.at[0], bias, T, 6 * g)
    keep_t[0] = T[0:384, :]
    keep_t[1] = T[1152:1536, :]
    bias = spread(bb, 3, 6)
    for g in range(6):
        last_layer(T, 6 * g, wp.at[1], bias, FS, 6 * g)
    gather_rows(FS, 4, 32, O)


def make_inner(enc, prior, w1, wd, wp, bb):
    return pl.pallas_call(
        inner_kernel,
        out_shape=(
            jax.ShapeDtypeStruct((32, 32, 256), BF16),
            jax.ShapeDtypeStruct((2, 2, 128, 256), BF16),
            jax.ShapeDtypeStruct((2, 256, 256), BF16),
            jax.ShapeDtypeStruct((2, 384, 256), BF16),
        ),
        in_specs=[vspec()] * 6,
        out_specs=(vspec(),) * 4,
        scratch_shapes=[
            VMEM((8, 128, 256), BF16),
            VMEM((3584, 256), BF16),
            VMEM((3584, 256), BF16),
            VMEM((1728, 256), BF16),
            VMEM((1536, 256), BF16),
            VMEM((2, 4, 288, 128), F32),
        ],
        compiler_params=pltpu.CompilerParams(vmem_limit_bytes=16 << 20),
        cost_estimate=pl.CostEstimate(
            flops=6_000_000_000, bytes_accessed=4_000_000, transcendentals=0
        ),
        name="middle",
    )(enc, prior, w1, wd, wp, bb)


def outer_kernel(
    enc, prior, inner, outer, w1, wd, wp, bb, keep_h, keep_d, keep_t, got, out,
    AF, HE, HO, D, T, FS, O, sems,
):
    copies = [pltpu.make_async_copy(got, out.at[0, 0, :, pl.ds(16, 32), :], sems.at[2])]
    copies[0].start()
    place = lax.axis_index("rows")
    is_top = lax.rem(place, 2) == 0
    keep_first = jnp.where(place == 0, 0.0, 1.0)
    keep_last = jnp.where(place == 31, 0.0, 1.0)
    zeros8 = jnp.zeros((8, 512), F32)
    for ch in range(2):
        a = inner[ch].astype(F32)
        b = outer[ch].astype(F32)
        above = jnp.where(is_top, b[8:16], a[8:16])
        below = jnp.where(is_top, a[0:8], b[0:8])
        fill(AF.at[0], ch, 0, jnp.concatenate([zeros8, above], axis=0))
        fill(AF.at[1], ch, 1, jnp.concatenate([below, zeros8], axis=0))
    fill(AF.at[0], 0, 1, enc[0:16, :].astype(F32))
    fill(AF.at[0], 1, 1, prior[0].astype(F32))
    fill(AF.at[1], 0, 0, enc[112:128, :].astype(F32))
    fill(AF.at[1], 1, 0, prior[7].astype(F32))
    bias = spread(bb, 0, 16)
    for phase, H in enumerate((HE, HO)):
        H[0, 512:640, :] = keep_h[phase, 0]
        H[1, 0:128, :] = keep_h[phase, 1]
    first_layer(AF.at[0], 0, w1, bias, HE.at[0], HO.at[0], 0, (keep_first, 0, 160))
    first_layer(AF.at[1], 0, w1, bias, HE.at[1], HO.at[1], 4, (keep_last, 160, 512))
    bias = spread(bb, 1, 3)
    D[0, 288:544, :] = keep_d[0]
    D[1, 0:256, :] = keep_d[1]
    for g in range(3):
        mask = (keep_first, 0, 64) if g == 0 else None
        down_layer(HE.at[0], HO.at[0], 6 * g, wd, bias, D.at[0], 3 * g, mask)
    for g in range(2):
        mask = (keep_last, 0, 96) if g == 1 else None
        down_layer(HE.at[1], HO.at[1], 6 * g + 2, wd, bias, D.at[1], 3 * g + 8, mask)
    bias = spread(bb, 2, 6)
    T[0, 384:768, :] = keep_t[0]
    T[1, 0:384, :] = keep_t[1]
    for g in range(2):
        mask = (keep_first, 0, 32) if g == 0 else None
        deep_layer(D.at[0], 6 * g, wp.at[0], bias, T.at[0], 6 * g, mask)
    deep_layer(D.at[1], 5, wp.at[0], bias, T.at[1], 12, (keep_last, 160, 192))
    T[1, 576:768, :] = jnp.zeros((192, 256), BF16)
    bias = spread(bb, 3, 6)
    for side in range(2):
        for g in range(3):
            last_layer(T.at[side], 6 * g, wp.at[1], bias, FS.at[side], 6 * g)
        gather_rows(FS.at[side], 0, 16, O.at[side])
        copy = pltpu.make_async_copy(
            O.at[side], out.at[0, 0, :, pl.ds(48 * side, 16), :], sems.at[side]
        )
        copy.start()
        copies.append(copy)
    for copy in copies:
        copy.wait()


def make_outer(enc, prior, inner, outer, w1, wd, wp, bb, keep_h, keep_d, keep_t, got):
    hbm = pl.BlockSpec(memory_space=pltpu.HBM)
    return pl.pallas_call(
        outer_kernel,
        out_shape=jax.ShapeDtypeStruct((1, 1, 32, 64, 256), BF16),
        in_specs=[vspec()] * 12,
        out_specs=hbm,
        scratch_shapes=[
            VMEM((2, 8, 32, 256), BF16),
            VMEM((2, 640, 256), BF16),
            VMEM((2, 640, 256), BF16),
            VMEM((2, 544, 256), BF16),
            VMEM((2, 768, 256), BF16),
            VMEM((2, 2, 4, 144, 128), F32),
            VMEM((2, 32, 16, 256), BF16),
            pltpu.SemaphoreType.DMA((3,)),
        ],
        compiler_params=pltpu.CompilerParams(vmem_limit_bytes=16 << 20),
        name="border",
    )(enc, prior, inner, outer, w1, wd, wp, bb, keep_h, keep_d, keep_t, got)


def pairs(target):
    return [(i, target(i)) for i in range(32) if 0 <= target(i) < 32]


SWAP = pairs(lambda i: i ^ 1)
OUTWARD = pairs(lambda i: i - 2 if i % 2 == 0 else i + 2)
INWARD = pairs(lambda i: i + 2 if i % 2 == 0 else i - 2)
LAST = [(i, t) for i, t in INWARD if i % 2 == 1]
ACROSS = pairs(lambda i: i - 1 if i % 2 == 0 else i + 1)


def per_device(
    sections, block_offset, row_base, col_base, fractions, blend,
    conv_first, bias_first, conv_down, bias_down, conv_deep, bias_deep,
):
    def send(value, route):
        return lax.ppermute(value, "rows", route)

    own = sections[0, 0]
    p1 = send(own, OUTWARD)
    p2 = send(own, INWARD)
    a = send(own, SWAP)
    f1 = send(p1, OUTWARD)
    f2 = send(p2, LAST)
    sp1 = send(p1, SWAP)
    sp2 = send(p2, SWAP)
    sf1 = send(f1, SWAP)
    w1, wd, wp, bb = make_weights(
        conv_first, conv_down, conv_deep, bias_first, bias_down, bias_deep
    )
    held = make_hold(own)
    pay, enc = make_warp(
        block_offset, row_base, col_base, fractions, blend,
        (held, a, p1, sp1, p2, sp2, f1, sf1, f2),
    )
    got = lax.all_to_all(pay, "gz", 0, 0)
    given = make_prior(got)
    prior = lax.all_to_all(given, "gz", 0, 0)
    edges = jnp.stack(
        [
            jnp.concatenate([enc[0:8], enc[120:128]], axis=0),
            jnp.concatenate([prior[0, 0:8], prior[7, 8:16]], axis=0),
        ]
    )
    inner = send(edges, SWAP)
    outer = send(edges, ACROSS)
    got, keep_h, keep_d, keep_t = make_inner(enc, prior, w1, wd, wp, bb)
    return make_outer(
        enc, prior, inner, outer, w1, wd, wp, bb, keep_h, keep_d, keep_t, got
    )


def solution(mesh):
    return jax.shard_map(
        per_device,
        mesh=mesh,
        in_specs=(
            P(None, "gz", "rows", None),
            P(None, "gz", "rows", None),
            P(None, "gz", "rows", None),
            P(None, "gz", "rows", None),
            P(None, None, "gz", "rows", None),
            P(None, "gz"),
            P(), P(), P(), P(), P(), P(),
        ),
        out_specs=P(None, "gz", None, "rows", None),
        check_vma=False,
    )
```
